256 devices in a mesh: grp: 4 (over y), col: 64 (over x, z, core).
Axes of the slice: x: 4, y: 4, z: 8, core: 2. Of those that a mesh axis runs over, the one named last changes fastest.
Arguments:
- inputs: bfloat16 [24, 256, 8192], P('grp', 'col'), may hold values from -6 to 6
- out_grads: bfloat16 [24, 256, 8192], P('grp', None, 'col'), may hold values from -0.5 to 0.5
- first_moment: float32 [8192, 8192], P(None, 'col'), may hold values from -2 to 2
- second_moment: float32 [8192, 8192], P(None, 'col'), may hold values from 0.01 to 1
- signs_in: int32 [8192], replicated, may hold values from 0 to 1
- signs_out: int32 [8192], replicated, may hold values from 0 to 1
- rows_in: int32 [64], replicated, may hold values from 0 to 8191, as said below
- rows_out: int32 [128], replicated, may hold values from 0 to 8191, as said below
- task_ids: int32 [24], P('grp'), may hold values from 0 to 7
- weights: int32 [24], P('grp'), may hold values from 1 to 4
Outputs:
- prototypes: float32 [8, 64, 128], P('grp', 'col')
The draws below stay inside these ranges and needn't reach their ends.
Inputs may be any that keep to these rules, and one draw needn't show every extreme that they name: `rows_in`: distinct row numbers. `rows_out`: distinct row numbers.
All inputs are finite; a program needn't handle non-finite values.
Results may differ from the reference program's by a relative error of at most 0.0019.
Values may be sent and summed in bfloat16 or wider, within the bound.
A program may use at most 128 MiB of HBM per device.

```python
import math
import jax
import jax.numpy as jnp
from jax import lax

D = 8192
TOK = 256
R1 = 64
R2 = 128
EXAMPLES = 24
NPROTO = 8


def draw_rows_in(key, part):
    return jax.random.permutation(jax.random.fold_in(key, 11), D)[:R1].astype(jnp.int32)


def draw_rows_out(key, part):
    return jax.random.permutation(jax.random.fold_in(key, 23), D)[:R2].astype(jnp.int32)


def with_ends(values, own_key, low, top_value):
    longest = values.shape.index(max(values.shape))
    spots = []
    for shift in (0, 1):
        where = [jax.random.randint(jax.random.fold_in(own_key, axis), (), 0, length) for axis, length in enumerate(values.shape)]
        where[longest] = (where[longest] + shift) % values.shape[longest]
        spots.append(tuple(where))
    return values.at[spots[0]].set(low).at[spots[1]].set(top_value)


def steps_of(own_key, dims, pieces, smallest, largest):
    level = 1.0
    for dim, shards_of in pieces:
        heights = jax.random.uniform(jax.random.fold_in(jax.random.fold_in(own_key, 6), dim), (shards_of,), jnp.float32, smallest / len(pieces), largest / len(pieces))
        level = level * jnp.repeat(jnp.exp(heights), dims[dim] // shards_of).reshape((-1,) + (1,) * (len(dims) - 1 - dim))
    return level


def normal_values(own_key, shape, spread, limit, pieces=(), held_as=jnp.bfloat16):
    values = jax.random.normal(own_key, shape, jnp.float32) * spread
    if len(pieces) > 0:
        values = steps_of(own_key, shape, pieces, -0.22, 0.18) * values
    return jnp.clip(values, min=-limit, max=limit).astype(held_as)


def setup_inputs(seed: int = 0) -> dict:
    splits = jax.random.split(jax.random.key(seed), 11)
    return {
        "inputs": normal_values(splits[0], (EXAMPLES, TOK, D), 1.0, 6.0, ((0, 4), (1, 64))),
        "out_grads": normal_values(splits[1], (EXAMPLES, TOK, D), 0.0625, 0.5, ((0, 4), (2, 64))),
        "first_moment": normal_values(splits[2], (D, D), 0.3, 2.0, ((1, 64),), jnp.float32),
        "second_moment": jnp.clip(jnp.exp(math.log(1.0) - 4.6051702 * jax.random.uniform(splits[3], (D, D), jnp.float32) ** steps_of(splits[3], (D, D), ((1, 64),), -0.2, 0.2)), 0.01, 1.0),
        "signs_in": with_ends(jax.random.randint(splits[4], (D,), 0, 2), jax.random.fold_in(splits[4], 1), 0, 1).astype(jnp.int32),
        "signs_out": with_ends(jax.random.randint(splits[5], (D,), 0, 2), jax.random.fold_in(splits[5], 1), 0, 1).astype(jnp.int32),
        "rows_in": draw_rows_in(jax.random.fold_in(splits[10], 71), 0),
        "rows_out": draw_rows_out(jax.random.fold_in(splits[10], 71), 0),
        "task_ids": with_ends(jax.random.randint(splits[8], (EXAMPLES,), 0, NPROTO), jax.random.fold_in(splits[8], 1), 0, NPROTO - 1).astype(jnp.int32),
        "weights": with_ends(jax.random.randint(splits[9], (EXAMPLES,), 1, 5), jax.random.fold_in(splits[9], 1), 1, 4).astype(jnp.int32),
    }


def hadamard_rows(rows, sign_bits):
    cols = jnp.arange(D, dtype=jnp.int32)
    both = jnp.bitwise_and(rows[:, None], cols[None, :])
    parity = jnp.zeros(both.shape, jnp.int32)
    for bit in range(int(math.log2(D)) + 1):
        parity = jnp.bitwise_xor(parity, jnp.bitwise_and(jnp.right_shift(both, bit), 1))
    value = (1 - 2 * parity) * (1 - 2 * sign_bits)[None, :]
    return value.astype(jnp.float32)

def reference(inputs, out_grads, first_moment, second_moment, signs_in, signs_out, rows_in, rows_out, task_ids, weights):
    left = hadamard_rows(rows_in, signs_in).astype(jnp.bfloat16)
    right = hadamard_rows(rows_out, signs_out)
    protos = jnp.arange(NPROTO, dtype=jnp.int32)

    def one(total, idx):
        grad = jnp.dot(inputs[idx].T, out_grads[idx], preferred_element_type=jnp.float32)
        first = 0.9 * first_moment + 0.1 * grad
        second = 0.999 * second_moment + 0.001 * grad * grad
        update = (first / (jnp.sqrt(second) + 1e-08)).astype(jnp.bfloat16)
        half = jnp.dot(left, update, preferred_element_type=jnp.float32)
        sketch = jnp.dot(half, right.T, precision=lax.Precision.HIGHEST)
        unit = sketch * lax.rsqrt(jnp.mean(sketch * sketch) + 1e-06)
        coef = jnp.where(protos == task_ids[idx], weights[idx].astype(jnp.float32), jnp.float32(0.0))
        return (total + coef[:, None, None] * unit[None], None)
    start = jnp.zeros((NPROTO, R1, R2), jnp.float32)
    total, _ = lax.scan(one, start, jnp.arange(EXAMPLES, dtype=jnp.int32))
    return total
```

```python
import functools
import math

import jax
import jax.numpy as jnp
from jax import lax
from jax.experimental import pallas as pl
from jax.experimental.pallas import tpu as pltpu
from jax.sharding import PartitionSpec as P

MESH = pl.DeviceIdType.MESH
F32 = jnp.float32
BF16 = jnp.bfloat16

NY = 4
NX = 4
NZ = 8
NCOL = NX * NZ * 2
EX = 6
EA = 3
TK = 4
D = 8192
QD = D // 4
CH = 256
NCH = QD // CH
SUB = CH // NY
C = 128
R1 = 64
R2 = 128
HALF = 128
PRO = 2

K_FM = 9.0 * math.sqrt(10.0)
K_G = math.sqrt(10.0)
K_SM = 999.0
K_EPS = 1e-8 * math.sqrt(1000.0)


def parity(both):
    for shift in (8, 4, 2, 1):
        both = jnp.bitwise_xor(both, jnp.right_shift(both, shift))
    return jnp.bitwise_and(both, 1)


def as_column(row, height):
    width = row.shape[1]
    r = lax.broadcasted_iota(jnp.int32, (height, width), 0)
    c = lax.broadcasted_iota(jnp.int32, (height, width), 1)
    return jnp.sum(jnp.where(r == c, jnp.broadcast_to(row, (height, width)), 0.0), axis=1, keepdims=True)


def as_row(column, width):
    height = column.shape[0]
    r = lax.broadcasted_iota(jnp.int32, (height, width), 0)
    c = lax.broadcasted_iota(jnp.int32, (height, width), 1)
    return jnp.sum(jnp.where(r == c, jnp.broadcast_to(column, (height, width)), 0.0), axis=0, keepdims=True)


def kernel(
    x_ref, og_ref, fm_ref, sm_ref, sin_ref, sout_ref, rin_ref, rout_ref, tid_ref, w_ref,
    out_ref,
    rx, xs, xg, ogb, ogt, fmb, smb, ta, tb, left_s, right_s, hacc, sk, rs, qs, qr, ts, yr,
    s_rx, s_rxs, s_ogl, s_og, s_ogs, s_ml, s_mc, s_mcs, s_mx, s_mxs, s_my, s_mys,
    s_ax, s_axs, s_az, s_azs, s_bz, s_bzs, s_bx, s_bxs,
    s_rs, s_rss, s_q, s_qs, s_t, s_tss,
):
    y = lax.axis_index("grp")
    me = lax.axis_index("col")
    core = lax.rem(me, 2)
    z = lax.rem(me // 2, NZ)
    x = me // (2 * NZ)
    pair = x // 2
    low = lax.rem(x, 2)
    cls = lax.rem(pair + low, 2)
    quarter = 2 * cls + core
    blk = 2 * low + core

    def col(x_, z_, c_):
        return (x_ * NZ + z_) * 2 + c_

    xpart = x + 1 - 2 * low
    cross = NX - 1 - x
    zp = lax.rem(z + 1, NZ)
    zm = lax.rem(z + NZ - 1, NZ)
    yp = lax.rem(y + 1, NY)
    ym = lax.rem(y + NY - 1, NY)
    d_core = (y, col(x, z, 1 - core))
    d_xp = tuple((y, col(xpart, z, c_)) for c_ in range(2))
    d_xsame = (y, col(xpart, z, core))
    d_cross = (y, col(cross, z, core))
    d_z = ((y, col(x, zp, core)), (y, col(x, zm, core)))
    d_y = ((yp, me), (ym, me))

    def remote(src, dst, ssem, rsem, dev):
        return pltpu.make_async_remote_copy(
            src_ref=src, dst_ref=dst, send_sem=ssem, recv_sem=rsem, device_id=dev, device_id_type=MESH
        )

    barrier = pltpu.get_barrier_semaphore()

    @pl.loop(1, NCOL)
    def _(k):
        pl.semaphore_signal(barrier, inc=1, device_id=(y, lax.rem(me + k, NCOL)), device_id_type=MESH)

    for k in range(1, NY):
        pl.semaphore_signal(barrier, inc=1, device_id=(lax.rem(y + k, NY), me), device_id_type=MESH)

    og_local = []
    for p_ in range(2):
        for l_ in range(2):
            cp = pltpu.make_async_copy(og_ref.at[:, p_, l_], ogb.at[blk, :, p_, :, l_], s_ogl.at[2 * p_ + l_])
            cp.start()
            og_local.append(cp)
    x_local = pltpu.make_async_copy(x_ref.at[:, :, pl.ds(pl.multiple_of(quarter * QD, QD), QD)], rx.at[blk], s_rx.at[blk])
    x_local.start()
    pl.semaphore_wait(barrier, NCOL - 1 + NY - 1)

    def x_send(dev, q, i):
        return remote(x_ref.at[:, :, pl.ds(pl.multiple_of(q * QD, QD), QD)], rx.at[blk], s_rxs.at[i], s_rx.at[blk], dev)

    x_sends = [
        x_send(d_xp[0], 2 * (1 - cls), 0),
        x_send(d_xp[1], 2 * (1 - cls) + 1, 1),
        x_send(d_core, 2 * cls + 1 - core, 2),
    ]
    for cp in x_sends:
        cp.start()
    for cp in og_local:
        cp.wait()
    og_core = remote(ogb.at[blk], ogb.at[blk], s_ogs.at[0], s_og.at[0], d_core)
    og_xp = remote(ogb.at[blk], ogb.at[blk], s_ogs.at[1], s_og.at[1], d_xsame)
    og_xp.start()
    og_core.start()

    rows_in = as_column(rin_ref[...].astype(F32), R1).astype(jnp.int32)
    rows_out = as_column(rout_ref[...].astype(F32), R2).astype(jnp.int32)

    @pl.loop(0, NCH)
    def _(j):
        tile = quarter * NCH + j
        cols = lax.broadcasted_iota(jnp.int32, (R1, CH), 1) + tile * CH
        bit = jnp.bitwise_xor(parity(jnp.bitwise_and(rows_in, cols)), jnp.broadcast_to(sin_ref[tile], (R1, CH)))
        left_s[j] = (1 - 2 * bit).astype(F32).astype(BF16)

    for b in range(4):
        owner = col(2 * pair + b // 2, z, b % 2)
        cols = lax.broadcasted_iota(jnp.int32, (R2, C), 1) + owner * C
        bit = jnp.bitwise_xor(parity(jnp.bitwise_and(rows_out, cols)), jnp.broadcast_to(sout_ref[owner], (R2, C)))
        right_s[:, b * C:(b + 1) * C] = (1 - 2 * bit).astype(F32).astype(BF16)

    hacc[...] = jnp.zeros_like(hacc)
    sk[...] = jnp.zeros_like(sk)

    for b in range(4):
        pltpu.make_async_copy(rx.at[b], rx.at[b], s_rx.at[b]).wait()
        xs[:, TK * b:TK * (b + 1), :] = rx[b].astype(F32)

    for j in range(NCH):
        xg[j, :, pair, z] = xs[:, :, j * CH:(j + 1) * CH].astype(BF16)

    A = slice(0, EA)
    B = slice(EA, EX)

    def zback(s, up):
        return lax.rem(z + NZ - (s - 1), NZ) if up == 0 else lax.rem(z + s - 1, NZ)

    def zcome(s, up):
        return lax.rem(z + NZ - s, NZ) if up == 0 else lax.rem(z + s, NZ)

    def a_x(j, where):
        v = xg.at[j, A, where, z]
        return remote(v, v, s_axs.at[j], s_ax.at[j], d_cross)

    def a_z(j, s, up, zz):
        v = xg.at[j, A, :, zz] if s < 4 else xg.at[j, A, :, zz, :, pl.ds(up * HALF, HALF)]
        return remote(v, v, s_azs.at[j, up, s - 1], s_az.at[j, up, s - 1], d_z[up])

    def b_z(j, s, up, zz):
        v = xg.at[j, B, pair, zz] if s < 4 else xg.at[j, B, pair, zz, :, pl.ds(up * HALF, HALF)]
        return remote(v, v, s_bzs.at[j, up, s - 1], s_bz.at[j, up, s - 1], d_z[up])

    def b_x(j, where):
        v = xg.at[j, B, where]
        return remote(v, v, s_bxs.at[j], s_bx.at[j], d_cross)

    moments = ((fm_ref, fmb), (sm_ref, smb))

    def rows(q, j, extra, n):
        return pl.ds(pl.multiple_of(q * QD + j * CH + extra, SUB), n)

    def m_local(j, a):
        return pltpu.make_async_copy(moments[a][0].at[rows(quarter, j, 0, CH)], moments[a][1].at[j, blk], s_ml.at[j, a])

    def m_core(j, a, b):
        q = 2 * cls + 1 - core
        return remote(moments[a][0].at[rows(q, j, 0, CH)], moments[a][1].at[j, b], s_mcs.at[j, a], s_mc.at[j, a], d_core)

    def m_x(j, a, h):
        q = 2 * (1 - cls) + h
        return remote(
            moments[a][0].at[rows(q, j, y * SUB, SUB)],
            moments[a][1].at[j, blk, pl.ds(pl.multiple_of(y * SUB, SUB), SUB)],
            s_mxs.at[j, a, h], s_mx.at[j, a, core], d_xp[h],
        )

    def m_x_come(j, a, h):
        v = moments[a][1].at[j, 2 * (1 - low) + h, pl.ds(pl.multiple_of(y * SUB, SUB), SUB)]
        return remote(v, v, s_mxs.at[j, a, h], s_mx.at[j, a, h], d_xp[h])

    def m_y(j, a, k, yy, up):
        v = moments[a][1].at[j, pl.ds(2 * (1 - low), 2), pl.ds(pl.multiple_of(yy * SUB, SUB), SUB)]
        return remote(v, v, s_mys.at[j, a, k], s_my.at[j, a, k], d_y[up])

    y2 = lax.rem(y + 2, NY)

    def stage(t, k, body):
        j = t - k

        @pl.when(jnp.logical_and(j >= 0, j < NCH))
        def _():
            body(j)

    def st5(j):
        for up in range(2):
            a_z(j, 4, up, zcome(4, up)).wait_recv()
        b_x(j, 1 - pair).wait_recv()

    def st4(j):
        for up in range(2):
            b_z(j, 4, up, zcome(4, up)).wait_recv()
        b_x(j, pair).start()
        for up in range(2):
            a_z(j, 3, up, zcome(3, up)).wait_recv()
            a_z(j, 4, up, zback(4, up)).start()

    def st3(j):
        for up in range(2):
            b_z(j, 3, up, zcome(3, up)).wait_recv()
            b_z(j, 4, up, zback(4, up)).start()
        for up in range(2):
            a_z(j, 2, up, zcome(2, up)).wait_recv()
            a_z(j, 3, up, zback(3, up)).start()

    def st2(j):
        for up in range(2):
            b_z(j, 2, up, zcome(2, up)).wait_recv()
            b_z(j, 3, up, zback(3, up)).start()
        for up in range(2):
            a_z(j, 1, up, zcome(1, up)).wait_recv()
            a_z(j, 2, up, zback(2, up)).start()
        m_y(j, 0, 0, ym, 0).wait_recv()
        m_y(j, 0, 2, ym, 0).start()
        m_y(j, 1, 1, yp, 1).wait_recv()
        m_y(j, 1, 2, yp, 1).start()

    def st1(j):
        for up in range(2):
            b_z(j, 1, up, zcome(1, up)).wait_recv()
            b_z(j, 2, up, zback(2, up)).start()
        a_x(j, 1 - pair).wait_recv()
        for up in range(2):
            a_z(j, 1, up, zback(1, up)).start()
        for a in range(2):
            for h in range(2):
                m_x_come(j, a, h).wait_recv()
            for up in range(2):
                m_y(j, a, up, y, up).start()

    def st0(j):
        a_x(j, pair).start()
        for up in range(2):
            b_z(j, 1, up, zback(1, up)).start()
        for a in range(2):
            for h in range(2):
                m_x(j, a, h).start()
        for a in range(2):
            m_core(j, a, blk).start()
            m_local(j, a).start()

    def compute(j):
        for a in range(2):
            m_y(j, a, 1 - a, (yp, ym)[a], 1 - a).wait_recv()
            m_y(j, a, 2, y2, a).wait_recv()
            m_core(j, a, 2 * low + 1 - core).wait_recv()
            m_local(j, a).wait()
        for b in range(4):
            ta[b * C:(b + 1) * C, :] = (fmb[j, b] * K_FM).T
            tb[b * C:(b + 1) * C, :] = (smb[j, b] * K_SM).T

        @pl.loop(0, EX)
        def _(e):
            acts = xg[j, e].reshape(2 * NZ * 4 * TK, CH)
            for h in range(2):
                sl = slice(h * 2 * C, (h + 1) * 2 * C)
                g = jnp.dot(ogt[e, sl, :], acts, preferred_element_type=F32)
                v = g * g + tb[sl, :]
                m = g * K_G + ta[sl, :]
                u = (m / (v * lax.rsqrt(v) + K_EPS)).astype(BF16)
                hacc[e, :, sl] += lax.dot_general(
                    left_s[j], u, (((1,), (1,)), ((), ())), preferred_element_type=F32
                )

    def og_forward():
        og_in = remote(ogb.at[2 * (1 - low) + core], ogb.at[2 * (1 - low) + core], s_ogs.at[1], s_og.at[1], d_xsame)
        og_in.wait_recv()
        remote(ogb.at[2 * (1 - low) + core], ogb.at[2 * (1 - low) + core], s_ogs.at[2], s_og.at[2], d_core).start()

    def og_finish():
        b1 = 2 * low + 1 - core
        b2 = 2 * (1 - low) + 1 - core
        remote(ogb.at[b1], ogb.at[b1], s_ogs.at[0], s_og.at[0], d_core).wait_recv()
        remote(ogb.at[b2], ogb.at[b2], s_ogs.at[2], s_og.at[2], d_core).wait_recv()

        @pl.loop(0, EX)
        def _(e):
            for b in range(4):
                v = ogb[b, e].astype(F32).reshape(4 * NZ * 8, C)
                ogt[e, b * C:(b + 1) * C, :] = v.T.astype(BF16)

    @pl.loop(0, NCH + 5)
    def _(t):
        stage(t, 5, st5)
        stage(t, 4, st4)
        stage(t, 3, st3)
        stage(t, 2, st2)
        stage(t, 1, st1)
        stage(t, 0, st0)

        @pl.when(t == 2)
        def _():
            og_forward()

        @pl.when(t == 4)
        def _():
            og_finish()

        stage(t, 5, compute)

    for e in range(EX):
        h = hacc[e]
        hi = h.astype(BF16)
        rest = h - hi.astype(F32)
        mid = rest.astype(BF16)
        lo = (rest - mid.astype(F32)).astype(BF16)
        dims = (((1,), (1,)), ((), ()))
        part = lax.dot_general(lo, right_s[...], dims, preferred_element_type=F32)
        part = part + lax.dot_general(mid, right_s[...], dims, preferred_element_type=F32)
        part = part + lax.dot_general(hi, right_s[...], dims, preferred_element_type=F32)
        sk[:, e, :] = part

    @pl.loop(1, NCOL)
    def _(k):
        to = lax.rem(me + k, NCOL)
        remote(sk.at[to], rs.at[me], s_rss, s_rs, (y, to)).start()

    rs[me] = sk[me]
    some = rs.at[pl.ds(0, NCOL - 1)]
    remote(some, some, s_rss, s_rs, d_core).wait_recv()
    rows_sum = jnp.sum(rs[...], axis=0)

    sq = as_row(jnp.sum(rows_sum * rows_sum, axis=1, keepdims=True), C)
    qs[...] = sq

    @pl.loop(1, NCOL)
    def _(k):
        to = lax.rem(me + k, NCOL)
        remote(qs, qr.at[me], s_qs, s_q, (y, to)).start()

    qr[me] = sq
    someq = qr.at[pl.ds(0, NCOL - 1)]
    remote(someq, someq, s_qs, s_q, d_core).wait_recv()
    squares = as_column(jnp.sum(qr[...], axis=0), 8)
    unit = rows_sum * lax.rsqrt(squares / (R1 * R2) + 1e-06)

    tid = as_column(tid_ref[...].astype(F32), 8)
    wgt = as_column(w_ref[...].astype(F32), 8)

    def term(p):
        coef = jnp.where(tid == p.astype(F32), wgt, 0.0)
        return jnp.sum(coef * unit, axis=0, keepdims=True)

    def terms(g):
        return jnp.concatenate([term(PRO * g + i) for i in range(PRO)], axis=0)

    y_sends = []
    for k in range(1, NY):
        g = lax.rem(y + k, NY)
        ts[k - 1] = terms(g)
        cp = remote(ts.at[k - 1], yr.at[k - 1], s_tss.at[k - 1], s_t.at[k - 1], (g, me))
        cp.start()
        y_sends.append(cp)
    total = terms(y)
    for cp in y_sends:
        cp.wait()
    out_ref[...] = total + (yr[0] + yr[1] + yr[2])

    remote(some, some, s_rss, s_rs, d_core).wait_send()
    remote(someq, someq, s_qs, s_q, d_core).wait_send()
    for cp in x_sends:
        cp.wait_send()
    og_core.wait_send()
    og_xp.wait_send()
    remote(ogb.at[2 * (1 - low) + core], ogb.at[2 * (1 - low) + core], s_ogs.at[2], s_og.at[2], d_core).wait_send()

    @pl.loop(0, NCH)
    def _(j):
        a_x(j, pair).wait_send()
        b_x(j, pair).wait_send()
        for up in range(2):
            for s in range(1, 5):
                a_z(j, s, up, zback(s, up)).wait_send()
                b_z(j, s, up, zback(s, up)).wait_send()
        for a in range(2):
            m_core(j, a, blk).wait_send()
            for h in range(2):
                m_x(j, a, h).wait_send()
            for up in range(2):
                m_y(j, a, up, y, up).wait_send()
        m_y(j, 0, 2, ym, 0).wait_send()
        m_y(j, 1, 2, yp, 1).wait_send()


def body(
    inputs,
    out_grads,
    first_moment,
    second_moment,
    signs_in,
    signs_out,
    rows_in,
    rows_out,
    task_ids,
    weights,
):
    hbm = pl.BlockSpec(memory_space=pl.ANY)
    vmem = pl.BlockSpec(memory_space=pltpu.VMEM)
    dma = pltpu.SemaphoreType.DMA
    out = pl.pallas_call(
        kernel,
        out_shape=jax.ShapeDtypeStruct((PRO, C), F32),
        in_specs=[hbm] * 4 + [vmem] * 6,
        out_specs=vmem,
        scratch_shapes=[
            pltpu.VMEM((4, EX, TK, QD), BF16),
            pltpu.VMEM((EX, 4 * TK, QD), F32),
            pltpu.VMEM((NCH, EX, 2, NZ, 4 * TK, CH), BF16),
            pltpu.VMEM((4, EX, 2, NZ, 2, 8, C), BF16),
            pltpu.VMEM((EX, 4 * C, 256), BF16),
            pltpu.VMEM((NCH, 4, CH, C), F32),
            pltpu.VMEM((NCH, 4, CH, C), F32),
            pltpu.VMEM((4 * C, CH), F32),
            pltpu.VMEM((4 * C, CH), F32),
            pltpu.VMEM((NCH, R1, CH), BF16),
            pltpu.VMEM((R2, 4 * C), BF16),
            pltpu.VMEM((EX, R1, 4 * C), F32),
            pltpu.VMEM((NCOL, 8, C), F32),
            pltpu.VMEM((NCOL, 8, C), F32),
            pltpu.VMEM((1, C), F32),
            pltpu.VMEM((NCOL, 1, C), F32),
            pltpu.VMEM((NY - 1, PRO, C), F32),
            pltpu.VMEM((NY - 1, PRO, C), F32),
            dma((4,)), dma((3,)),
            dma((4,)), dma((3,)), dma((3,)),
            dma((NCH, 2)),
            dma((NCH, 2)), dma((NCH, 2)),
            dma((NCH, 2, 2)), dma((NCH, 2, 2)),
            dma((NCH, 2, 3)), dma((NCH, 2, 3)),
            dma((NCH,)), dma((NCH,)),
            dma((NCH, 2, 4)), dma((NCH, 2, 4)),
            dma((NCH, 2, 4)), dma((NCH, 2, 4)),
            dma((NCH,)), dma((NCH,)),
            dma, dma, dma, dma,
            dma((NY - 1,)), dma((NY - 1,)),
        ],
        compiler_params=pltpu.CompilerParams(
            collective_id=0, has_side_effects=True, vmem_limit_bytes=60 * 1024 * 1024
        ),
    )(
        inputs,
        out_grads.reshape(EX, 2, 2, NZ, 8, C),
        first_moment,
        second_moment,
        signs_in.reshape(D // CH, 1, CH),
        signs_out.reshape(NCOL, 1, C),
        rows_in.reshape(1, R1),
        rows_out.reshape(1, R2),
        task_ids.reshape(1, EX),
        weights.reshape(1, EX),
    )
    return out.reshape(PRO, 1, C)


def solution(mesh):
    placed = (
        P("grp", "col", None),
        P("grp", None, "col"),
        P(None, "col"),
        P(None, "col"),
        P(),
        P(),
        P(),
        P(),
        P("grp"),
        P("grp"),
    )
    return jax.shard_map(
        body, mesh=mesh, in_specs=placed, out_specs=P("grp", "col", None), check_vma=False
    )
```

```python
import functools
import math

import jax
import jax.numpy as jnp
from jax import lax
from jax.experimental import pallas as pl
from jax.experimental.pallas import tpu as pltpu
from jax.sharding import PartitionSpec as P

MESH = pl.DeviceIdType.MESH
F32 = jnp.float32
BF16 = jnp.bfloat16

NY = 4
NX = 4
NZ = 8
NCHIP = NX * NZ
NCOL = NCHIP * 2
EX = 6
EA = 3
TK = 4
D = 8192
QD = D // 4
CH = 256
NCH = QD // CH
MFIRST = 3
SUB = CH // NY
C = 128
R1 = 64
R2 = 128
HALF = 128
PRO = 2

K_FM = 9.0 * math.sqrt(10.0)
K_G = math.sqrt(10.0)
K_SM = 999.0
K_EPS = 1e-8 * math.sqrt(1000.0)


def parity(both):
    for shift in (8, 4, 2, 1):
        both = jnp.bitwise_xor(both, jnp.right_shift(both, shift))
    return jnp.bitwise_and(both, 1)


def as_column(row, height):
    width = row.shape[1]
    r = lax.broadcasted_iota(jnp.int32, (height, width), 0)
    c = lax.broadcasted_iota(jnp.int32, (height, width), 1)
    return jnp.sum(jnp.where(r == c, jnp.broadcast_to(row, (height, width)), 0.0), axis=1, keepdims=True)


def as_row(column, width):
    height = column.shape[0]
    r = lax.broadcasted_iota(jnp.int32, (height, width), 0)
    c = lax.broadcasted_iota(jnp.int32, (height, width), 1)
    return jnp.sum(jnp.where(r == c, jnp.broadcast_to(column, (height, width)), 0.0), axis=0, keepdims=True)


def kernel(
    x_ref, og_ref, fm_ref, sm_ref, sin_hbm, sout_hbm, rin_hbm, rout_hbm, tid_hbm, w_hbm,
    out_ref,
    sin_ref, sout_ref, rin_ref, rout_ref, tid_ref, w_ref, s_small,
    rx, xs, xg, ogb, ogt, fmb, smb, ta, tb, left_s, right_s, hacc, sk, sc, rs, qs, qr, ts, yr,
    s_rx, s_rxs, s_ogl, s_og, s_ogs, s_ml, s_mc, s_mcs, s_mx, s_mxs, s_my, s_mys,
    s_ax, s_axs, s_az, s_azs, s_bz, s_bzs, s_bx, s_bxs,
    s_sc, s_scs, s_rs, s_rss, s_q, s_qs, s_t, s_tss,
):
    y = lax.axis_index("grp")
    me = lax.axis_index("col")
    core = lax.rem(me, 2)
    z = lax.rem(me // 2, NZ)
    x = me // (2 * NZ)
    pair = x // 2
    low = lax.rem(x, 2)
    cls = lax.rem(pair + low, 2)
    quarter = 2 * cls + core
    blk = 2 * low + core

    def col(x_, z_, c_):
        return (x_ * NZ + z_) * 2 + c_

    xpart = x + 1 - 2 * low
    cross = NX - 1 - x
    zp = lax.rem(z + 1, NZ)
    zm = lax.rem(z + NZ - 1, NZ)
    yp = lax.rem(y + 1, NY)
    ym = lax.rem(y + NY - 1, NY)
    d_core = (y, col(x, z, 1 - core))
    d_xp = tuple((y, col(xpart, z, c_)) for c_ in range(2))
    d_xsame = (y, col(xpart, z, core))
    d_cross = (y, col(cross, z, core))
    d_z = ((y, col(x, zp, core)), (y, col(x, zm, core)))
    d_y = ((yp, me), (ym, me))

    def remote(src, dst, ssem, rsem, dev):
        return pltpu.make_async_remote_copy(
            src_ref=src, dst_ref=dst, send_sem=ssem, recv_sem=rsem, device_id=dev, device_id_type=MESH
        )

    barrier = pltpu.get_barrier_semaphore()
    for dev in (d_core, *d_xp, d_cross, *d_z, *d_y):
        pl.semaphore_signal(barrier, inc=1, device_id=dev, device_id_type=MESH)

    og_local = []
    for p_ in range(2):
        for l_ in range(2):
            cp = pltpu.make_async_copy(og_ref.at[:, p_, l_], ogb.at[blk, :, p_, :, l_], s_ogl.at[2 * p_ + l_])
            cp.start()
            og_local.append(cp)
    def x_part(q, j):
        return x_ref.at[:, :, pl.ds(pl.multiple_of(q * QD + j * CH, CH), CH)]

    def x_local(j):
        return pltpu.make_async_copy(x_part(quarter, j), rx.at[j, blk], s_rx.at[j, blk])

    def x_sends(j):
        targets = ((d_xp[0], 2 * (1 - cls)), (d_xp[1], 2 * (1 - cls) + 1), (d_core, 2 * cls + 1 - core))
        return [remote(x_part(q, j), rx.at[j, blk], s_rxs.at[j, i], s_rx.at[j, blk], dev) for i, (dev, q) in enumerate(targets)]

    @pl.loop(0, NCH)
    def _(j):
        x_local(j).start()

    small = []
    for i, (src, dst) in enumerate(
        ((sin_hbm, sin_ref), (sout_hbm, sout_ref), (rin_hbm, rin_ref), (rout_hbm, rout_ref), (tid_hbm, tid_ref), (w_hbm, w_ref))
    ):
        cp = pltpu.make_async_copy(src, dst, s_small.at[i])
        cp.start()
        small.append(cp)
    pl.semaphore_wait(barrier, 8)

    @pl.loop(0, NCH)
    def _(j):
        for cp in x_sends(j):
            cp.start()

    A = slice(0, EA)
    B = slice(EA, EX)

    def zback(s, up):
        return lax.rem(z + NZ - (s - 1), NZ) if up == 0 else lax.rem(z + s - 1, NZ)

    def zcome(s, up):
        return lax.rem(z + NZ - s, NZ) if up == 0 else lax.rem(z + s, NZ)

    def own_x(j, where):
        v = xg.at[j, :, where, z]
        return remote(v, v, s_axs.at[j], s_ax.at[j], d_cross)

    def a_z(j, s, up, zz):
        v = xg.at[j, A, :, zz] if s < 4 else xg.at[j, A, :, zz, :, pl.ds(up * HALF, HALF)]
        return remote(v, v, s_azs.at[j, up, s - 1], s_az.at[j, up, s - 1], d_z[up])

    def b_z(j, s, up, zz):
        v = xg.at[j, B, pair, zz] if s < 4 else xg.at[j, B, pair, zz, :, pl.ds(up * HALF, HALF)]
        return remote(v, v, s_bzs.at[j, up, s - 1], s_bz.at[j, up, s - 1], d_z[up])

    def b_x(j, n, where, zz):
        v = xg.at[j, B, where, zz]
        return remote(v, v, s_bxs.at[j, n], s_bx.at[j, n], d_cross)

    moments = ((fm_ref, fmb), (sm_ref, smb))

    def rows(q, j, extra, n):
        return pl.ds(pl.multiple_of(q * QD + j * CH + extra, SUB), n)

    def m_local(j, a):
        return pltpu.make_async_copy(moments[a][0].at[rows(quarter, j, 0, CH)], moments[a][1].at[j, blk], s_ml.at[j, a])

    def m_core(j, a, b):
        q = 2 * cls + 1 - core
        return remote(moments[a][0].at[rows(q, j, 0, CH)], moments[a][1].at[j, b], s_mcs.at[j, a], s_mc.at[j, a], d_core)

    def m_x(j, a, h):
        q = 2 * (1 - cls) + h
        return remote(
            moments[a][0].at[rows(q, j, y * SUB, SUB)],
            moments[a][1].at[j, blk, pl.ds(pl.multiple_of(y * SUB, SUB), SUB)],
            s_mxs.at[j, a, h], s_mx.at[j, a, core], d_xp[h],
        )

    def m_x_come(j, a, h):
        v = moments[a][1].at[j, 2 * (1 - low) + h, pl.ds(pl.multiple_of(y * SUB, SUB), SUB)]
        return remote(v, v, s_mxs.at[j, a, h], s_mx.at[j, a, h], d_xp[h])

    def m_y(j, a, k, yy, up):
        v = moments[a][1].at[j, pl.ds(2 * (1 - low), 2), pl.ds(pl.multiple_of(yy * SUB, SUB), SUB)]
        return remote(v, v, s_mys.at[j, a, k], s_my.at[j, a, k], d_y[up])

    y2 = lax.rem(y + 2, NY)

    def m_start(j):
        for a in range(2):
            for h in range(2):
                m_x(j, a, h).start()
        for a in range(2):
            m_core(j, a, blk).start()
            m_local(j, a).start()

    def stage(t, k, body):
        j = t - k

        @pl.when(jnp.logical_and(j >= 0, j < NCH))
        def _():
            body(j)

    def st5(j):
        for up in range(2):
            a_z(j, 4, up, zcome(4, up)).wait_recv()

    def st4(j):
        for up in range(2):
            b_z(j, 4, up, zcome(4, up)).wait_recv()
        b_x(j, 6, pair, zcome(4, 0)).start()
        for up in range(2):
            a_z(j, 3, up, zcome(3, up)).wait_recv()
            a_z(j, 4, up, zback(4, up)).start()

    def st_b(j, s):
        for up in range(2):
            b_z(j, s, up, zcome(s, up)).wait_recv()
            b_z(j, s + 1, up, zback(s + 1, up)).start()
            b_x(j, 2 * (s - 1) + up, pair, zcome(s, up)).start()

    def st3(j):
        st_b(j, 3)
        for up in range(2):
            a_z(j, 2, up, zcome(2, up)).wait_recv()
            a_z(j, 3, up, zback(3, up)).start()

    def st2(j):
        st_b(j, 2)
        for up in range(2):
            a_z(j, 1, up, zcome(1, up)).wait_recv()
            a_z(j, 2, up, zback(2, up)).start()
        m_y(j, 0, 0, ym, 0).wait_recv()
        m_y(j, 0, 2, ym, 0).start()
        m_y(j, 1, 1, yp, 1).wait_recv()
        m_y(j, 1, 2, yp, 1).start()

    def st1(j):
        st_b(j, 1)
        own_x(j, 1 - pair).wait_recv()
        for up in range(2):
            a_z(j, 1, up, zback(1, up)).start()
        for a in range(2):
            for h in range(2):
                m_x_come(j, a, h).wait_recv()
            for up in range(2):
                m_y(j, a, up, y, up).start()

    def st0(j):
        for b in range(4):
            pltpu.make_async_copy(rx.at[j, b], rx.at[j, b], s_rx.at[j, b]).wait()
            xs[:, TK * b:TK * (b + 1), :] = rx[j, b].astype(F32)
        xg[j, :, pair, z] = xs[...].astype(BF16)
        own_x(j, pair).start()
        for up in range(2):
            b_z(j, 1, up, zback(1, up)).start()

    def compute(j):
        for a in range(2):
            m_y(j, a, 1 - a, (yp, ym)[a], 1 - a).wait_recv()
            m_y(j, a, 2, y2, a).wait_recv()
            m_core(j, a, 2 * low + 1 - core).wait_recv()
            m_local(j, a).wait()
        for n in range(6):
            b_x(j, n, 1 - pair, zcome(n // 2 + 1, n % 2)).wait_recv()
        b_x(j, 6, 1 - pair, zcome(4, 0)).wait_recv()
        for b in range(4):
            ta[b * C:(b + 1) * C, :] = (fmb[j, b] * K_FM).T
            tb[b * C:(b + 1) * C, :] = (smb[j, b] * K_SM).T

        @pl.loop(0, EX)
        def _(e):
            acts = xg[j, e].reshape(2 * NZ * 4 * TK, CH)
            for h in range(2):
                sl = slice(h * 2 * C, (h + 1) * 2 * C)
                g = jnp.dot(ogt[e, sl, :], acts, preferred_element_type=F32)
                v = g * g + tb[sl, :]
                m = g * K_G + ta[sl, :]
                u = (m / (v * lax.rsqrt(v) + K_EPS)).astype(BF16)
                hacc[e, :, sl] += lax.dot_general(
                    left_s[j], u, (((1,), (1,)), ((), ())), preferred_element_type=F32
                )

    def og_forward():
        og_in = remote(ogb.at[2 * (1 - low) + core], ogb.at[2 * (1 - low) + core], s_ogs.at[1], s_og.at[1], d_xsame)
        og_in.wait_recv()
        remote(ogb.at[2 * (1 - low) + core], ogb.at[2 * (1 - low) + core], s_ogs.at[2], s_og.at[2], d_core).start()

    def og_finish():
        b1 = 2 * low + 1 - core
        b2 = 2 * (1 - low) + 1 - core
        remote(ogb.at[b1], ogb.at[b1], s_ogs.at[0], s_og.at[0], d_core).wait_recv()
        remote(ogb.at[b2], ogb.at[b2], s_ogs.at[2], s_og.at[2], d_core).wait_recv()

        @pl.loop(0, EX)
        def _(e):
            for b in range(4):
                v = ogb[b, e].astype(F32).reshape(4 * NZ * 8, C)
                ogt[e, b * C:(b + 1) * C, :] = v.T.astype(BF16)

    pl.loop(0, MFIRST)(m_start)
    for cp in og_local:
        cp.wait()
    og_core = remote(ogb.at[blk], ogb.at[blk], s_ogs.at[0], s_og.at[0], d_core)
    og_xp = remote(ogb.at[blk], ogb.at[blk], s_ogs.at[1], s_og.at[1], d_xsame)

    og_xp.start()
    og_core.start()
    pl.loop(MFIRST, NCH)(m_start)

    for cp in small:
        cp.wait()
    r = lax.broadcasted_iota(jnp.int32, (R1, R1), 0)
    c = lax.broadcasted_iota(jnp.int32, (R1, R1), 1)
    spread = jnp.where(2 * lax.rem(r, NCHIP) + r // NCHIP == c, jnp.broadcast_to(rin_ref[...].astype(F32), (R1, R1)), 0.0)
    rows_in = jnp.sum(spread, axis=1, keepdims=True).astype(jnp.int32)
    rows_out = as_column(rout_ref[...].astype(F32), R2).astype(jnp.int32)

    @pl.loop(0, NCH)
    def _(j):
        tile = quarter * NCH + j
        cols = lax.broadcasted_iota(jnp.int32, (R1, CH), 1) + tile * CH
        bit = jnp.bitwise_xor(parity(jnp.bitwise_and(rows_in, cols)), jnp.broadcast_to(sin_ref[tile], (R1, CH)))
        left_s[j] = (1 - 2 * bit).astype(F32).astype(BF16)

    for b in range(4):
        owner = col(2 * pair + b // 2, z, b % 2)
        cols = lax.broadcasted_iota(jnp.int32, (R2, C), 1) + owner * C
        bit = jnp.bitwise_xor(parity(jnp.bitwise_and(rows_out, cols)), jnp.broadcast_to(sout_ref[owner], (R2, C)))
        right_s[:, b * C:(b + 1) * C] = (1 - 2 * bit).astype(F32).astype(BF16)

    hacc[...] = jnp.zeros_like(hacc)
    sk[...] = jnp.zeros_like(sk)

    @pl.loop(0, NCH + 5)
    def _(t):
        stage(t, 5, st5)
        stage(t, 4, st4)
        stage(t, 3, st3)
        stage(t, 2, st2)
        stage(t, 1, st1)
        stage(t, 0, st0)

        @pl.when(t == 2)
        def _():
            og_forward()

        @pl.when(t == 4)
        def _():
            og_finish()

        stage(t, 5, compute)

    for e in range(EX):
        h = hacc[e]
        hi = h.astype(BF16)
        rest = h - hi.astype(F32)
        mid = rest.astype(BF16)
        lo = (rest - mid.astype(F32)).astype(BF16)
        dims = (((1,), (1,)), ((), ()))
        part = lax.dot_general(lo, right_s[...], dims, preferred_element_type=F32)
        part = part + lax.dot_general(mid, right_s[...], dims, preferred_element_type=F32)
        part = part + lax.dot_general(hi, right_s[...], dims, preferred_element_type=F32)
        sk[:, e, :] = part

    to_core = remote(
        sk.at[pl.ds(pl.multiple_of((1 - core) * NCHIP, NCHIP), NCHIP)], sc, s_scs, s_sc, d_core
    )
    to_core.start()
    hops = sorted(((min(i, NX - i) + min(k, NZ - k), i, k) for i in range(NX) for k in range(NZ)), reverse=True)
    xt = [lax.rem(x + i, NX) * NZ for i in range(NX)]
    zt = [lax.rem(z + i, NZ) for i in range(NZ)]
    others = [xt[i] + zt[k] for _, i, k in hops if i or k]
    chip = me // 2
    to_core.wait()
    sc[...] += sk[pl.ds(pl.multiple_of(core * NCHIP, NCHIP), NCHIP)]
    for to in others:
        remote(sc.at[to], rs.at[chip], s_rss, s_rs, (y, to * 2 + core)).start()

    rs[chip] = sc[chip]
    some = rs.at[pl.ds(0, NCHIP - 1)]
    remote(some, some, s_rss, s_rs, d_core).wait_recv()
    rows_sum = jnp.sum(rs[...], axis=0)

    sq = as_row(jnp.sum(rows_sum * rows_sum, axis=1, keepdims=True), C)
    qs[...] = sq

    for to in others:
        for c_ in (1 - core, core):
            remote(qs, qr.at[me], s_qs, s_q, (y, to * 2 + c_)).start()
    remote(qs, qr.at[me], s_qs, s_q, d_core).start()

    qr[me] = sq
    someq = qr.at[pl.ds(0, NCOL - 1)]
    remote(someq, someq, s_qs, s_q, d_core).wait_recv()
    squares = as_column(jnp.sum(qr[...], axis=0), 8)
    unit = rows_sum * lax.rsqrt(squares / (R1 * R2) + 1e-06)

    tid = as_column(tid_ref[...].astype(F32), 8)
    wgt = as_column(w_ref[...].astype(F32), 8)

    def term(p):
        coef = jnp.where(tid == p.astype(F32), wgt, 0.0)
        return jnp.sum(coef * unit, axis=0, keepdims=True)

    def terms(g):
        return jnp.concatenate([term(PRO * g + i) for i in range(PRO)], axis=0)

    y_sends = []
    for k in range(1, NY):
        g = lax.rem(y + k, NY)
        ts[k - 1] = terms(g)
        cp = remote(ts.at[k - 1], yr.at[k - 1], s_tss.at[k - 1], s_t.at[k - 1], (g, me))
        cp.start()
        y_sends.append(cp)
    total = terms(y)
    for cp in y_sends:
        cp.wait()
    out_ref[...] = total + (yr[0] + yr[1] + yr[2])

    remote(some, some, s_rss, s_rs, d_core).wait_send()
    remote(someq, someq, s_qs, s_q, d_core).wait_send()
    og_core.wait_send()
    og_xp.wait_send()
    remote(ogb.at[2 * (1 - low) + core], ogb.at[2 * (1 - low) + core], s_ogs.at[2], s_og.at[2], d_core).wait_send()

    @pl.loop(0, NCH)
    def _(j):
        for cp in x_sends(j):
            cp.wait_send()
        own_x(j, pair).wait_send()
        for n in range(6):
            b_x(j, n, pair, zcome(n // 2 + 1, n % 2)).wait_send()
        b_x(j, 6, pair, zcome(4, 0)).wait_send()
        for up in range(2):
            for s in range(1, 5):
                a_z(j, s, up, zback(s, up)).wait_send()
                b_z(j, s, up, zback(s, up)).wait_send()
        for a in range(2):
            m_core(j, a, blk).wait_send()
            for h in range(2):
                m_x(j, a, h).wait_send()
            for up in range(2):
                m_y(j, a, up, y, up).wait_send()
        m_y(j, 0, 2, ym, 0).wait_send()
        m_y(j, 1, 2, yp, 1).wait_send()


def body(
    inputs,
    out_grads,
    first_moment,
    second_moment,
    signs_in,
    signs_out,
    rows_in,
    rows_out,
    task_ids,
    weights,
):
    hbm = pl.BlockSpec(memory_space=pl.ANY)
    vmem = pl.BlockSpec(memory_space=pltpu.VMEM)
    dma = pltpu.SemaphoreType.DMA
    out = pl.pallas_call(
        kernel,
        out_shape=jax.ShapeDtypeStruct((PRO, C), F32),
        in_specs=[hbm] * 10,
        out_specs=vmem,
        scratch_shapes=[
            pltpu.VMEM((D // CH, 1, CH), jnp.int32),
            pltpu.VMEM((NCOL, 1, C), jnp.int32),
            pltpu.VMEM((1, R1), jnp.int32),
            pltpu.VMEM((1, R2), jnp.int32),
            pltpu.VMEM((1, EX), jnp.int32),
            pltpu.VMEM((1, EX), jnp.int32),
            dma((6,)),
            pltpu.VMEM((NCH, 4, EX, TK, CH), BF16),
            pltpu.VMEM((EX, 4 * TK, CH), F32),
            pltpu.VMEM((NCH, EX, 2, NZ, 4 * TK, CH), BF16),
            pltpu.VMEM((4, EX, 2, NZ, 2, 8, C), BF16),
            pltpu.VMEM((EX, 4 * C, 256), BF16),
            pltpu.VMEM((NCH, 4, CH, C), F32),
            pltpu.VMEM((NCH, 4, CH, C), F32),
            pltpu.VMEM((4 * C, CH), F32),
            pltpu.VMEM((4 * C, CH), F32),
            pltpu.VMEM((NCH, R1, CH), BF16),
            pltpu.VMEM((R2, 4 * C), BF16),
            pltpu.VMEM((EX, R1, 4 * C), F32),
            pltpu.VMEM((NCOL, 8, C), F32),
            pltpu.VMEM((NCHIP, 8, C), F32),
            pltpu.VMEM((NCHIP, 8, C), F32),
            pltpu.VMEM((1, C), F32),
            pltpu.VMEM((NCOL, 1, C), F32),
            pltpu.VMEM((NY - 1, PRO, C), F32),
            pltpu.VMEM((NY - 1, PRO, C), F32),
            dma((NCH, 4)), dma((NCH, 3)),
            dma((4,)), dma((3,)), dma((3,)),
            dma((NCH, 2)),
            dma((NCH, 2)), dma((NCH, 2)),
            dma((NCH, 2, 2)), dma((NCH, 2, 2)),
            dma((NCH, 2, 3)), dma((NCH, 2, 3)),
            dma((NCH,)), dma((NCH,)),
            dma((NCH, 2, 4)), dma((NCH, 2, 4)),
            dma((NCH, 2, 4)), dma((NCH, 2, 4)),
            dma((NCH, 7)), dma((NCH, 7)),
            dma, dma, dma, dma, dma, dma,
            dma((NY - 1,)), dma((NY - 1,)),
        ],
        compiler_params=pltpu.CompilerParams(
            collective_id=0, has_side_effects=True, vmem_limit_bytes=60 * 1024 * 1024
        ),
    )(
        inputs,
        out_grads.reshape(EX, 2, 2, NZ, 8, C),
        first_moment,
        second_moment,
        signs_in.reshape(D // CH, 1, CH),
        signs_out.reshape(NCOL, 1, C),
        rows_in.reshape(1, R1),
        rows_out.reshape(1, R2),
        task_ids.reshape(1, EX),
        weights.reshape(1, EX),
    )
    return out.reshape(PRO, 1, C)


def solution(mesh):
    placed = (
        P("grp", "col", None),
        P("grp", None, "col"),
        P(None, "col"),
        P(None, "col"),
        P(),
        P(),
        P(),
        P(),
        P("grp"),
        P("grp"),
    )
    return jax.shard_map(
        body, mesh=mesh, in_specs=placed, out_specs=P("grp", "col", None), check_vma=False
    )
```

```python
import functools
import math

import jax
import jax.numpy as jnp
from jax import lax
from jax.experimental import pallas as pl
from jax.experimental.pallas import tpu as pltpu
from jax.sharding import PartitionSpec as P

MESH = pl.DeviceIdType.MESH
F32 = jnp.float32
BF16 = jnp.bfloat16

NY = 4
NX = 4
NZ = 8
NCHIP = NX * NZ
NCOL = NCHIP * 2
EX = 6
EA = 3
TK = 4
D = 8192
QD = D // 4
CH = 256
NCH = QD // CH
MFIRST = 3
Y_OWN = 2
OG_ON = 4
OG_END = 5
SUB = CH // NY
C = 128
R1 = 64
R2 = 128
HALF = 128
PRO = 2

K_FM = 9.0 * math.sqrt(10.0)
K_G = math.sqrt(10.0)
K_SM = 999.0
K_EPS = 1e-8 * math.sqrt(1000.0)


def parity(both):
    for shift in (8, 4, 2, 1):
        both = jnp.bitwise_xor(both, jnp.right_shift(both, shift))
    return jnp.bitwise_and(both, 1)


def as_column(row, height):
    width = row.shape[1]
    r = lax.broadcasted_iota(jnp.int32, (height, width), 0)
    c = lax.broadcasted_iota(jnp.int32, (height, width), 1)
    return jnp.sum(jnp.where(r == c, jnp.broadcast_to(row, (height, width)), 0.0), axis=1, keepdims=True)


def as_row(column, width):
    height = column.shape[0]
    r = lax.broadcasted_iota(jnp.int32, (height, width), 0)
    c = lax.broadcasted_iota(jnp.int32, (height, width), 1)
    return jnp.sum(jnp.where(r == c, jnp.broadcast_to(column, (height, width)), 0.0), axis=0, keepdims=True)


def kernel(
    x_ref, og_ref, fm_ref, sm_ref, sin_hbm, sout_hbm, rin_hbm, rout_hbm, tid_hbm, w_hbm,
    out_ref,
    sin_ref, sout_ref, rin_ref, rout_ref, tid_ref, w_ref, s_small,
    rx, xs, xg, ogb, ogt, fmb, smb, ta, tb, left_s, right_s, hacc, sk, sc, rs, qs, qr, ts, yr,
    s_rx, s_rxs, s_ogl, s_og, s_ogs, s_ml, s_mc, s_mcs, s_mx, s_mxs, s_my, s_mys,
    s_ax, s_axs, s_az, s_azs, s_bz, s_bzs, s_bx, s_bxs,
    s_sc, s_scs, s_rs, s_rss, s_q, s_qs, s_t, s_tss,
):
    y = lax.axis_index("grp")
    me = lax.axis_index("col")
    core = lax.rem(me, 2)
    z = lax.rem(me // 2, NZ)
    x = me // (2 * NZ)
    pair = x // 2
    low = lax.rem(x, 2)
    cls = lax.rem(pair + low, 2)
    quarter = 2 * cls + core
    blk = 2 * low + core

    def col(x_, z_, c_):
        return (x_ * NZ + z_) * 2 + c_

    xpart = x + 1 - 2 * low
    cross = NX - 1 - x
    zp = lax.rem(z + 1, NZ)
    zm = lax.rem(z + NZ - 1, NZ)
    yp = lax.rem(y + 1, NY)
    ym = lax.rem(y + NY - 1, NY)
    d_core = (y, col(x, z, 1 - core))
    d_xp = tuple((y, col(xpart, z, c_)) for c_ in range(2))
    d_xsame = (y, col(xpart, z, core))
    d_cross = (y, col(cross, z, core))
    d_z = ((y, col(x, zp, core)), (y, col(x, zm, core)))
    d_y = ((yp, me), (ym, me))

    def remote(src, dst, ssem, rsem, dev):
        return pltpu.make_async_remote_copy(
            src_ref=src, dst_ref=dst, send_sem=ssem, recv_sem=rsem, device_id=dev, device_id_type=MESH
        )

    barrier = pltpu.get_barrier_semaphore()
    for dev in (d_core, *d_xp, d_cross, *d_z, *d_y):
        pl.semaphore_signal(barrier, inc=1, device_id=dev, device_id_type=MESH)

    og_local = []
    for p_ in range(2):
        for l_ in range(2):
            cp = pltpu.make_async_copy(og_ref.at[:, p_, l_], ogb.at[blk, :, p_, :, l_], s_ogl.at[2 * p_ + l_])
            cp.start()
            og_local.append(cp)
    def x_part(q, j):
        return x_ref.at[:, :, pl.ds(pl.multiple_of(q * QD + j * CH, CH), CH)]

    def x_local(j):
        return pltpu.make_async_copy(x_part(quarter, j), rx.at[j, blk], s_rx.at[j, blk])

    def x_sends(j):
        targets = ((d_xp[0], 2 * (1 - cls)), (d_xp[1], 2 * (1 - cls) + 1), (d_core, 2 * cls + 1 - core))
        return [remote(x_part(q, j), rx.at[j, blk], s_rxs.at[j, i], s_rx.at[j, blk], dev) for i, (dev, q) in enumerate(targets)]

    @pl.loop(0, NCH)
    def _(j):
        x_local(j).start()

    small = []
    for i, (src, dst) in enumerate(
        ((sin_hbm, sin_ref), (sout_hbm, sout_ref), (rin_hbm, rin_ref), (rout_hbm, rout_ref), (tid_hbm, tid_ref), (w_hbm, w_ref))
    ):
        cp = pltpu.make_async_copy(src, dst, s_small.at[i])
        cp.start()
        small.append(cp)
    pl.semaphore_wait(barrier, 8)

    @pl.loop(0, NCH)
    def _(j):
        for cp in x_sends(j):
            cp.start()

    A = slice(0, EA)
    B = slice(EA, EX)

    def zback(s, up):
        return lax.rem(z + NZ - (s - 1), NZ) if up == 0 else lax.rem(z + s - 1, NZ)

    def zcome(s, up):
        return lax.rem(z + NZ - s, NZ) if up == 0 else lax.rem(z + s, NZ)

    def own_x(j, where):
        v = xg.at[j, :, where, z]
        return remote(v, v, s_axs.at[j], s_ax.at[j], d_cross)

    def a_z(j, s, up, zz):
        v = xg.at[j, A, :, zz] if s < 4 else xg.at[j, A, :, zz, :, pl.ds(up * HALF, HALF)]
        return remote(v, v, s_azs.at[j, up, s - 1], s_az.at[j, up, s - 1], d_z[up])

    def b_z(j, s, up, zz):
        v = xg.at[j, B, pair, zz] if s < 4 else xg.at[j, B, pair, zz, :, pl.ds(up * HALF, HALF)]
        return remote(v, v, s_bzs.at[j, up, s - 1], s_bz.at[j, up, s - 1], d_z[up])

    def b_x(j, n, where, zz):
        v = xg.at[j, B, where, zz]
        return remote(v, v, s_bxs.at[j, n], s_bx.at[j, n], d_cross)

    moments = ((fm_ref, fmb), (sm_ref, smb))

    def rows(q, j, extra, n):
        return pl.ds(pl.multiple_of(q * QD + j * CH + extra, SUB), n)

    def m_local(j, a):
        return pltpu.make_async_copy(moments[a][0].at[rows(quarter, j, 0, CH)], moments[a][1].at[j, blk], s_ml.at[j, a])

    def m_core(j, a, b):
        q = 2 * cls + 1 - core
        return remote(moments[a][0].at[rows(q, j, 0, CH)], moments[a][1].at[j, b], s_mcs.at[j, a], s_mc.at[j, a], d_core)

    def m_x(j, a, h):
        q = 2 * (1 - cls) + h
        return remote(
            moments[a][0].at[rows(q, j, y * SUB, SUB)],
            moments[a][1].at[j, blk, pl.ds(pl.multiple_of(y * SUB, SUB), SUB)],
            s_mxs.at[j, a, h], s_mx.at[j, a, core], d_xp[h],
        )

    def m_x_come(j, a, h):
        v = moments[a][1].at[j, 2 * (1 - low) + h, pl.ds(pl.multiple_of(y * SUB, SUB), SUB)]
        return remote(v, v, s_mxs.at[j, a, h], s_mx.at[j, a, h], d_xp[h])

    def m_y(j, a, k, yy, up):
        v = moments[a][1].at[j, pl.ds(2 * (1 - low), 2), pl.ds(pl.multiple_of(yy * SUB, SUB), SUB)]
        return remote(v, v, s_mys.at[j, a, k], s_my.at[j, a, k], d_y[up])

    y2 = lax.rem(y + 2, NY)

    def m_start(j):
        for a in range(2):
            for h in range(2):
                m_x(j, a, h).start()
        for a in range(2):
            m_core(j, a, blk).start()
            m_local(j, a).start()

    def stage(t, k, body):
        j = t - k

        @pl.when(jnp.logical_and(j >= 0, j < NCH))
        def _():
            body(j)

    def a_step(s):
        def go(j):
            if s == 1:
                own_x(j, 1 - pair).wait_recv()
            for up in range(2):
                if s > 1:
                    a_z(j, s - 1, up, zcome(s - 1, up)).wait_recv()
                if s < 5:
                    a_z(j, s, up, zback(s, up)).start()

        return go

    def b_step(s):
        def go(j):
            for up in range(2):
                if s > 1:
                    b_z(j, s - 1, up, zcome(s - 1, up)).wait_recv()
                if s < 5:
                    b_z(j, s, up, zback(s, up)).start()
                if 1 < s < 5:
                    b_x(j, 2 * (s - 2) + up, pair, zcome(s - 1, up)).start()
            if s == 5:
                b_x(j, 6, pair, zcome(4, 0)).start()

        return go

    def own_piece(j):
        for b in range(4):
            pltpu.make_async_copy(rx.at[j, b], rx.at[j, b], s_rx.at[j, b]).wait()
            xs[:, TK * b:TK * (b + 1), :] = rx[j, b].astype(F32)
        xg[j, :, pair, z] = xs[...].astype(BF16)
        own_x(j, pair).start()

    def y_own(j):
        for a in range(2):
            for h in range(2):
                m_x_come(j, a, h).wait_recv()
            for up in range(2):
                m_y(j, a, up, y, up).start()

    def y_on(j):
        m_y(j, 0, 0, ym, 0).wait_recv()
        m_y(j, 0, 2, ym, 0).start()
        m_y(j, 1, 1, yp, 1).wait_recv()
        m_y(j, 1, 2, yp, 1).start()

    def compute(j):
        for a in range(2):
            m_y(j, a, 1 - a, (yp, ym)[a], 1 - a).wait_recv()
            m_y(j, a, 2, y2, a).wait_recv()
            m_core(j, a, 2 * low + 1 - core).wait_recv()
            m_local(j, a).wait()
        for n in range(6):
            b_x(j, n, 1 - pair, zcome(n // 2 + 1, n % 2)).wait_recv()
        b_x(j, 6, 1 - pair, zcome(4, 0)).wait_recv()
        for b in range(4):
            ta[b * C:(b + 1) * C, :] = (fmb[j, b] * K_FM).T
            tb[b * C:(b + 1) * C, :] = (smb[j, b] * K_SM).T

        def one(e):
            acts = xg[j, e].reshape(2 * NZ * 4 * TK, CH)
            for h in range(2):
                sl = slice(h * 2 * C, (h + 1) * 2 * C)
                g = jnp.dot(ogt[e, sl, :], acts, preferred_element_type=F32)
                v = g * g + tb[sl, :]
                m = g * K_G + ta[sl, :]
                u = (m / (v * lax.rsqrt(v) + K_EPS)).astype(BF16)
                hacc[e, :, sl] += lax.dot_general(
                    left_s[j], u, (((1,), (1,)), ((), ())), preferred_element_type=F32
                )

        for e in range(EX):
            one(e)

    def og_forward():
        og_in = remote(ogb.at[2 * (1 - low) + core], ogb.at[2 * (1 - low) + core], s_ogs.at[1], s_og.at[1], d_xsame)
        og_in.wait_recv()
        remote(ogb.at[2 * (1 - low) + core], ogb.at[2 * (1 - low) + core], s_ogs.at[2], s_og.at[2], d_core).start()

    def og_finish():
        b1 = 2 * low + 1 - core
        b2 = 2 * (1 - low) + 1 - core
        remote(ogb.at[b1], ogb.at[b1], s_ogs.at[0], s_og.at[0], d_core).wait_recv()
        remote(ogb.at[b2], ogb.at[b2], s_ogs.at[2], s_og.at[2], d_core).wait_recv()

        @pl.loop(0, EX)
        def _(e):
            for b in range(4):
                v = ogb[b, e].astype(F32).reshape(4 * NZ * 8, C)
                ogt[e, b * C:(b + 1) * C, :] = v.T.astype(BF16)

    pl.loop(0, MFIRST)(m_start)
    for cp in og_local:
        cp.wait()
    og_core = remote(ogb.at[blk], ogb.at[blk], s_ogs.at[0], s_og.at[0], d_core)
    og_xp = remote(ogb.at[blk], ogb.at[blk], s_ogs.at[1], s_og.at[1], d_xsame)

    og_xp.start()
    og_core.start()
    pl.loop(MFIRST, NCH)(m_start)

    for cp in small:
        cp.wait()
    r = lax.broadcasted_iota(jnp.int32, (R1, R1), 0)
    c = lax.broadcasted_iota(jnp.int32, (R1, R1), 1)
    spread = jnp.where(2 * lax.rem(r, NCHIP) + r // NCHIP == c, jnp.broadcast_to(rin_ref[...].astype(F32), (R1, R1)), 0.0)
    rows_in = jnp.sum(spread, axis=1, keepdims=True).astype(jnp.int32)
    rows_out = as_column(rout_ref[...].astype(F32), R2).astype(jnp.int32)

    @pl.loop(0, NCH)
    def _(j):
        tile = quarter * NCH + j
        cols = lax.broadcasted_iota(jnp.int32, (R1, CH), 1) + tile * CH
        bit = jnp.bitwise_xor(parity(jnp.bitwise_and(rows_in, cols)), jnp.broadcast_to(sin_ref[tile], (R1, CH)))
        left_s[j] = (1 - 2 * bit).astype(F32).astype(BF16)

    for b in range(4):
        owner = col(2 * pair + b // 2, z, b % 2)
        cols = lax.broadcasted_iota(jnp.int32, (R2, C), 1) + owner * C
        bit = jnp.bitwise_xor(parity(jnp.bitwise_and(rows_out, cols)), jnp.broadcast_to(sout_ref[owner], (R2, C)))
        right_s[:, b * C:(b + 1) * C] = (1 - 2 * bit).astype(F32).astype(BF16)

    hacc[...] = jnp.zeros_like(hacc)
    sk[...] = jnp.zeros_like(sk)

    @pl.loop(0, NCH + 5)
    def _(t):
        for s in (5, 4, 3, 2, 1):
            stage(t, s, a_step(s))
        stage(t, 0, own_piece)
        stage(t, Y_OWN, y_own)
        for s in (5, 4, 3, 2, 1):
            stage(t, s - 1, b_step(s))
        stage(t, Y_OWN + 1, y_on)

        @pl.when(t == OG_ON)
        def _():
            og_forward()

        @pl.when(t == OG_END)
        def _():
            og_finish()

        stage(t, 5, compute)

    for e in range(EX):
        h = hacc[e]
        hi = h.astype(BF16)
        rest = h - hi.astype(F32)
        mid = rest.astype(BF16)
        lo = (rest - mid.astype(F32)).astype(BF16)
        dims = (((1,), (1,)), ((), ()))
        part = lax.dot_general(lo, right_s[...], dims, preferred_element_type=F32)
        part = part + lax.dot_general(mid, right_s[...], dims, preferred_element_type=F32)
        part = part + lax.dot_general(hi, right_s[...], dims, preferred_element_type=F32)
        sk[:, e, :] = part

    to_core = remote(
        sk.at[pl.ds(pl.multiple_of((1 - core) * NCHIP, NCHIP), NCHIP)], sc, s_scs, s_sc, d_core
    )
    to_core.start()
    hops = sorted(((min(i, NX - i) + min(k, NZ - k), i, k) for i in range(NX) for k in range(NZ)), reverse=True)
    xt = [lax.rem(x + i, NX) * NZ for i in range(NX)]
    zt = [lax.rem(z + i, NZ) for i in range(NZ)]
    others = [xt[i] + zt[k] for _, i, k in hops if i or k]
    chip = me // 2
    to_core.wait()
    sc[...] += sk[pl.ds(pl.multiple_of(core * NCHIP, NCHIP), NCHIP)]
    for to in others:
        remote(sc.at[to], rs.at[chip], s_rss, s_rs, (y, to * 2 + core)).start()

    rs[chip] = sc[chip]
    some = rs.at[pl.ds(0, NCHIP - 1)]
    remote(some, some, s_rss, s_rs, d_core).wait_recv()
    rows_sum = jnp.sum(rs[...], axis=0)

    sq = as_row(jnp.sum(rows_sum * rows_sum, axis=1, keepdims=True), C)
    qs[...] = sq

    for to in others:
        for c_ in (1 - core, core):
            remote(qs, qr.at[me], s_qs, s_q, (y, to * 2 + c_)).start()
    remote(qs, qr.at[me], s_qs, s_q, d_core).start()

    qr[me] = sq
    someq = qr.at[pl.ds(0, NCOL - 1)]
    remote(someq, someq, s_qs, s_q, d_core).wait_recv()
    squares = as_column(jnp.sum(qr[...], axis=0), 8)
    unit = rows_sum * lax.rsqrt(squares / (R1 * R2) + 1e-06)

    tid = as_column(tid_ref[...].astype(F32), 8)
    wgt = as_column(w_ref[...].astype(F32), 8)

    def term(p):
        coef = jnp.where(tid == p.astype(F32), wgt, 0.0)
        return jnp.sum(coef * unit, axis=0, keepdims=True)

    def terms(g):
        return jnp.concatenate([term(PRO * g + i) for i in range(PRO)], axis=0)

    y_sends = []
    for k in range(1, NY):
        g = lax.rem(y + k, NY)
        ts[k - 1] = terms(g)
        cp = remote(ts.at[k - 1], yr.at[k - 1], s_tss.at[k - 1], s_t.at[k - 1], (g, me))
        cp.start()
        y_sends.append(cp)
    total = terms(y)
    for cp in y_sends:
        cp.wait()
    out_ref[...] = total + (yr[0] + yr[1] + yr[2])

    remote(some, some, s_rss, s_rs, d_core).wait_send()
    remote(someq, someq, s_qs, s_q, d_core).wait_send()
    og_core.wait_send()
    og_xp.wait_send()
    remote(ogb.at[2 * (1 - low) + core], ogb.at[2 * (1 - low) + core], s_ogs.at[2], s_og.at[2], d_core).wait_send()

    @pl.loop(0, NCH)
    def _(j):
        for cp in x_sends(j):
            cp.wait_send()
        own_x(j, pair).wait_send()
        for n in range(6):
            b_x(j, n, pair, zcome(n // 2 + 1, n % 2)).wait_send()
        b_x(j, 6, pair, zcome(4, 0)).wait_send()
        for up in range(2):
            for s in range(1, 5):
                a_z(j, s, up, zback(s, up)).wait_send()
                b_z(j, s, up, zback(s, up)).wait_send()
        for a in range(2):
            m_core(j, a, blk).wait_send()
            for h in range(2):
                m_x(j, a, h).wait_send()
            for up in range(2):
                m_y(j, a, up, y, up).wait_send()
        m_y(j, 0, 2, ym, 0).wait_send()
        m_y(j, 1, 2, yp, 1).wait_send()


def body(
    inputs,
    out_grads,
    first_moment,
    second_moment,
    signs_in,
    signs_out,
    rows_in,
    rows_out,
    task_ids,
    weights,
):
    hbm = pl.BlockSpec(memory_space=pl.ANY)
    vmem = pl.BlockSpec(memory_space=pltpu.VMEM)
    dma = pltpu.SemaphoreType.DMA
    out = pl.pallas_call(
        kernel,
        out_shape=jax.ShapeDtypeStruct((PRO, C), F32),
        in_specs=[hbm] * 10,
        out_specs=vmem,
        scratch_shapes=[
            pltpu.VMEM((D // CH, 1, CH), jnp.int32),
            pltpu.VMEM((NCOL, 1, C), jnp.int32),
            pltpu.VMEM((1, R1), jnp.int32),
            pltpu.VMEM((1, R2), jnp.int32),
            pltpu.VMEM((1, EX), jnp.int32),
            pltpu.VMEM((1, EX), jnp.int32),
            dma((6,)),
            pltpu.VMEM((NCH, 4, EX, TK, CH), BF16),
            pltpu.VMEM((EX, 4 * TK, CH), F32),
            pltpu.VMEM((NCH, EX, 2, NZ, 4 * TK, CH), BF16),
            pltpu.VMEM((4, EX, 2, NZ, 2, 8, C), BF16),
            pltpu.VMEM((EX, 4 * C, 256), BF16),
            pltpu.VMEM((NCH, 4, CH, C), F32),
            pltpu.VMEM((NCH, 4, CH, C), F32),
            pltpu.VMEM((4 * C, CH), F32),
            pltpu.VMEM((4 * C, CH), F32),
            pltpu.VMEM((NCH, R1, CH), BF16),
            pltpu.VMEM((R2, 4 * C), BF16),
            pltpu.VMEM((EX, R1, 4 * C), F32),
            pltpu.VMEM((NCOL, 8, C), F32),
            pltpu.VMEM((NCHIP, 8, C), F32),
            pltpu.VMEM((NCHIP, 8, C), F32),
            pltpu.VMEM((1, C), F32),
            pltpu.VMEM((NCOL, 1, C), F32),
            pltpu.VMEM((NY - 1, PRO, C), F32),
            pltpu.VMEM((NY - 1, PRO, C), F32),
            dma((NCH, 4)), dma((NCH, 3)),
            dma((4,)), dma((3,)), dma((3,)),
            dma((NCH, 2)),
            dma((NCH, 2)), dma((NCH, 2)),
            dma((NCH, 2, 2)), dma((NCH, 2, 2)),
            dma((NCH, 2, 3)), dma((NCH, 2, 3)),
            dma((NCH,)), dma((NCH,)),
            dma((NCH, 2, 4)), dma((NCH, 2, 4)),
            dma((NCH, 2, 4)), dma((NCH, 2, 4)),
            dma((NCH, 7)), dma((NCH, 7)),
            dma, dma, dma, dma, dma, dma,
            dma((NY - 1,)), dma((NY - 1,)),
        ],
        compiler_params=pltpu.CompilerParams(
            collective_id=0, has_side_effects=True, vmem_limit_bytes=60 * 1024 * 1024
        ),
    )(
        inputs,
        out_grads.reshape(EX, 2, 2, NZ, 8, C),
        first_moment,
        second_moment,
        signs_in.reshape(D // CH, 1, CH),
        signs_out.reshape(NCOL, 1, C),
        rows_in.reshape(1, R1),
        rows_out.reshape(1, R2),
        task_ids.reshape(1, EX),
        weights.reshape(1, EX),
    )
    return out.reshape(PRO, 1, C)


def solution(mesh):
    placed = (
        P("grp", "col", None),
        P("grp", None, "col"),
        P(None, "col"),
        P(None, "col"),
        P(),
        P(),
        P(),
        P(),
        P("grp"),
        P("grp"),
    )
    return jax.shard_map(
        body, mesh=mesh, in_specs=placed, out_specs=P("grp", "col", None), check_vma=False
    )
```

```python
import functools
import math

import jax
import jax.numpy as jnp
from jax import lax
from jax.experimental import pallas as pl
from jax.experimental.pallas import tpu as pltpu
from jax.sharding import PartitionSpec as P

MESH = pl.DeviceIdType.MESH
F32 = jnp.float32
BF16 = jnp.bfloat16

NY = 4
NX = 4
NZ = 8
NCHIP = NX * NZ
NCOL = NCHIP * 2
EX = 6
TK = 4
D = 8192
QD = D // 4
CH = 256
NCH = QD // CH
MFIRST = 6
EA = (3, 2, 3, 2, 3, 2, 3, 2)
FIRST = (0, 0, 1, 1, 2, 2, 3, 3)
Y_OWN = 2
OG_ON = 4
OG_END = 5
SUB = CH // NY
C = 128
R1 = 64
R2 = 128
HALF = 128
PRO = 2

K_FM = 9.0 * math.sqrt(10.0)
K_G = math.sqrt(10.0)
K_SM = 999.0
K_EPS = 1e-8 * math.sqrt(1000.0)


def parity(both):
    for shift in (8, 4, 2, 1):
        both = jnp.bitwise_xor(both, jnp.right_shift(both, shift))
    return jnp.bitwise_and(both, 1)


def as_column(row, height):
    width = row.shape[1]
    r = lax.broadcasted_iota(jnp.int32, (height, width), 0)
    c = lax.broadcasted_iota(jnp.int32, (height, width), 1)
    return jnp.sum(jnp.where(r == c, jnp.broadcast_to(row, (height, width)), 0.0), axis=1, keepdims=True)


def as_row(column, width):
    height = column.shape[0]
    r = lax.broadcasted_iota(jnp.int32, (height, width), 0)
    c = lax.broadcasted_iota(jnp.int32, (height, width), 1)
    return jnp.sum(jnp.where(r == c, jnp.broadcast_to(column, (height, width)), 0.0), axis=0, keepdims=True)


def kernel(
    x_ref, og_ref, fm_ref, sm_ref, sin_hbm, sout_hbm, rin_hbm, rout_hbm, tid_hbm, w_hbm,
    out_ref,
    sin_ref, sout_ref, rin_ref, rout_ref, tid_ref, w_ref, s_small,
    rx, xs, xg, ogb, ogt, fmb, smb, ta, tb, left_s, right_s, hacc, sk, sc, rs, qs, qr, ts, yr,
    s_rx, s_rxs, s_ogl, s_og, s_ogs, s_ml, s_mc, s_mcs, s_mx, s_mxs, s_my, s_mys,
    s_ax, s_axs, s_az, s_azs, s_bz, s_bzs, s_bx, s_bxs,
    s_sc, s_scs, s_rs, s_rss, s_q, s_qs, s_t, s_tss,
):
    y = lax.axis_index("grp")
    me = lax.axis_index("col")
    core = lax.rem(me, 2)
    z = lax.rem(me // 2, NZ)
    x = me // (2 * NZ)
    pair = x // 2
    low = lax.rem(x, 2)
    cls = lax.rem(pair + low, 2)
    quarter = 2 * cls + core
    blk = 2 * low + core

    def col(x_, z_, c_):
        return (x_ * NZ + z_) * 2 + c_

    xpart = x + 1 - 2 * low
    cross = NX - 1 - x
    zp = lax.rem(z + 1, NZ)
    zm = lax.rem(z + NZ - 1, NZ)
    yp = lax.rem(y + 1, NY)
    ym = lax.rem(y + NY - 1, NY)
    d_core = (y, col(x, z, 1 - core))
    d_xp = tuple((y, col(xpart, z, c_)) for c_ in range(2))
    d_xsame = (y, col(xpart, z, core))
    d_cross = (y, col(cross, z, core))
    d_z = ((y, col(x, zp, core)), (y, col(x, zm, core)))
    d_y = ((yp, me), (ym, me))

    def remote(src, dst, ssem, rsem, dev):
        return pltpu.make_async_remote_copy(
            src_ref=src, dst_ref=dst, send_sem=ssem, recv_sem=rsem, device_id=dev, device_id_type=MESH
        )

    barrier = pltpu.get_barrier_semaphore()
    for dev in (d_core, *d_xp, d_cross, *d_z, *d_y):
        pl.semaphore_signal(barrier, inc=1, device_id=dev, device_id_type=MESH)

    og_local = []
    for p_ in range(2):
        for l_ in range(2):
            cp = pltpu.make_async_copy(og_ref.at[:, p_, l_], ogb.at[blk, :, p_, :, l_], s_ogl.at[2 * p_ + l_])
            cp.start()
            og_local.append(cp)
    def x_part(q, j):
        return x_ref.at[:, :, pl.ds(pl.multiple_of(q * QD + j * CH, CH), CH)]

    def x_local(j):
        return pltpu.make_async_copy(x_part(quarter, j), rx.at[j, blk], s_rx.at[j, blk])

    def x_sends(j):
        targets = ((d_xp[0], 2 * (1 - cls)), (d_xp[1], 2 * (1 - cls) + 1), (d_core, 2 * cls + 1 - core))
        return [remote(x_part(q, j), rx.at[j, blk], s_rxs.at[j, i], s_rx.at[j, blk], dev) for i, (dev, q) in enumerate(targets)]

    @pl.loop(0, NCH)
    def _(j):
        x_local(j).start()

    small = []
    for i, (src, dst) in enumerate(
        ((sin_hbm, sin_ref), (sout_hbm, sout_ref), (rin_hbm, rin_ref), (rout_hbm, rout_ref), (tid_hbm, tid_ref), (w_hbm, w_ref))
    ):
        cp = pltpu.make_async_copy(src, dst, s_small.at[i])
        cp.start()
        small.append(cp)
    pl.semaphore_wait(barrier, 8)

    @pl.loop(0, NCH)
    def _(j):
        for cp in x_sends(j):
            cp.start()

    def A(j):
        return slice(0, EA[j])

    def B(j):
        return slice(EA[j], EX)

    def zback(s, up):
        return lax.rem(z + NZ - (s - 1), NZ) if up == 0 else lax.rem(z + s - 1, NZ)

    def zcome(s, up):
        return lax.rem(z + NZ - s, NZ) if up == 0 else lax.rem(z + s, NZ)

    def own_x(j, where):
        v = xg.at[j, :, where, z]
        return remote(v, v, s_axs.at[j], s_ax.at[j], d_cross)

    def a_z(j, s, up, zz):
        v = xg.at[j, A(j), :, zz] if s < 4 else xg.at[j, A(j), :, zz, :, pl.ds(up * HALF, HALF)]
        return remote(v, v, s_azs.at[j, up, s - 1], s_az.at[j, up, s - 1], d_z[up])

    def b_z(j, s, up, zz):
        v = xg.at[j, B(j), pair, zz] if s < 4 else xg.at[j, B(j), pair, zz, :, pl.ds(up * HALF, HALF)]
        return remote(v, v, s_bzs.at[j, up, s - 1], s_bz.at[j, up, s - 1], d_z[up])

    def b_x(j, n, where, zz):
        v = xg.at[j, B(j), where, zz]
        return remote(v, v, s_bxs.at[j, n], s_bx.at[j, n], d_cross)

    moments = ((fm_ref, fmb), (sm_ref, smb))

    def rows(q, j, extra, n):
        return pl.ds(pl.multiple_of(q * QD + j * CH + extra, SUB), n)

    def m_local(j, a):
        return pltpu.make_async_copy(moments[a][0].at[rows(quarter, j, 0, CH)], moments[a][1].at[j, blk], s_ml.at[j, a])

    def m_core(j, a, b):
        q = 2 * cls + 1 - core
        return remote(moments[a][0].at[rows(q, j, 0, CH)], moments[a][1].at[j, b], s_mcs.at[j, a], s_mc.at[j, a], d_core)

    def m_x(j, a, h):
        q = 2 * (1 - cls) + h
        return remote(
            moments[a][0].at[rows(q, j, y * SUB, SUB)],
            moments[a][1].at[j, blk, pl.ds(pl.multiple_of(y * SUB, SUB), SUB)],
            s_mxs.at[j, a, h], s_mx.at[j, a, core], d_xp[h],
        )

    def m_x_come(j, a, h):
        v = moments[a][1].at[j, 2 * (1 - low) + h, pl.ds(pl.multiple_of(y * SUB, SUB), SUB)]
        return remote(v, v, s_mxs.at[j, a, h], s_mx.at[j, a, h], d_xp[h])

    def m_y(j, a, k, yy, up):
        v = moments[a][1].at[j, pl.ds(2 * (1 - low), 2), pl.ds(pl.multiple_of(yy * SUB, SUB), SUB)]
        return remote(v, v, s_mys.at[j, a, k], s_my.at[j, a, k], d_y[up])

    y2 = lax.rem(y + 2, NY)

    def m_start(j):
        for a in range(2):
            for h in range(2):
                m_x(j, a, h).start()
        for a in range(2):
            m_core(j, a, blk).start()
            m_local(j, a).start()

    def a_step(s):
        def go(j):
            if s == 1:
                own_x(j, 1 - pair).wait_recv()
            for up in range(2):
                if s > 1:
                    a_z(j, s - 1, up, zcome(s - 1, up)).wait_recv()
                if s < 5:
                    a_z(j, s, up, zback(s, up)).start()

        return go

    def b_step(s):
        def go(j):
            for up in range(2):
                if s > 1:
                    b_z(j, s - 1, up, zcome(s - 1, up)).wait_recv()
                if s < 5:
                    b_z(j, s, up, zback(s, up)).start()
                if 1 < s < 5:
                    b_x(j, 2 * (s - 2) + up, pair, zcome(s - 1, up)).start()
            if s == 5:
                b_x(j, 6, pair, zcome(4, 0)).start()

        return go

    def own_piece(j):
        for b in range(4):
            pltpu.make_async_copy(rx.at[j, b], rx.at[j, b], s_rx.at[j, b]).wait()
            xs[:, TK * b:TK * (b + 1), :] = rx[j, b].astype(F32)
        xg[j, :, pair, z] = xs[...].astype(BF16)
        own_x(j, pair).start()

    def y_own(j):
        for a in range(2):
            for h in range(2):
                m_x_come(j, a, h).wait_recv()
            for up in range(2):
                m_y(j, a, up, y, up).start()

    def y_on(j):
        m_y(j, 0, 0, ym, 0).wait_recv()
        m_y(j, 0, 2, ym, 0).start()
        m_y(j, 1, 1, yp, 1).wait_recv()
        m_y(j, 1, 2, yp, 1).start()

    def compute(j):
        for a in range(2):
            m_y(j, a, 1 - a, (yp, ym)[a], 1 - a).wait_recv()
            m_y(j, a, 2, y2, a).wait_recv()
            m_core(j, a, 2 * low + 1 - core).wait_recv()
            m_local(j, a).wait()
        for n in range(6):
            b_x(j, n, 1 - pair, zcome(n // 2 + 1, n % 2)).wait_recv()
        b_x(j, 6, 1 - pair, zcome(4, 0)).wait_recv()
        for b in range(4):
            ta[b * C:(b + 1) * C, :] = (fmb[j, b] * K_FM).T
            tb[b * C:(b + 1) * C, :] = (smb[j, b] * K_SM).T

        def one(e):
            acts = xg[j, e].reshape(2 * NZ * 4 * TK, CH)
            for h in range(2):
                sl = slice(h * 2 * C, (h + 1) * 2 * C)
                g = jnp.dot(ogt[e, sl, :], acts, preferred_element_type=F32)
                v = g * g + tb[sl, :]
                m = g * K_G + ta[sl, :]
                u = (m / (v * lax.rsqrt(v) + K_EPS)).astype(BF16)
                hacc[e, :, sl] += lax.dot_general(
                    left_s[j], u, (((1,), (1,)), ((), ())), preferred_element_type=F32
                )

        for e in range(EX):
            one(e)

    def og_forward():
        og_in = remote(ogb.at[2 * (1 - low) + core], ogb.at[2 * (1 - low) + core], s_ogs.at[1], s_og.at[1], d_xsame)
        og_in.wait_recv()
        remote(ogb.at[2 * (1 - low) + core], ogb.at[2 * (1 - low) + core], s_ogs.at[2], s_og.at[2], d_core).start()

    def og_finish():
        b1 = 2 * low + 1 - core
        b2 = 2 * (1 - low) + 1 - core
        remote(ogb.at[b1], ogb.at[b1], s_ogs.at[0], s_og.at[0], d_core).wait_recv()
        remote(ogb.at[b2], ogb.at[b2], s_ogs.at[2], s_og.at[2], d_core).wait_recv()

        @pl.loop(0, EX)
        def _(e):
            for b in range(4):
                v = ogb[b, e].astype(F32).reshape(4 * NZ * 8, C)
                ogt[e, b * C:(b + 1) * C, :] = v.T.astype(BF16)

    pl.loop(0, MFIRST)(m_start)
    for cp in og_local:
        cp.wait()
    og_core = remote(ogb.at[blk], ogb.at[blk], s_ogs.at[0], s_og.at[0], d_core)
    og_xp = remote(ogb.at[blk], ogb.at[blk], s_ogs.at[1], s_og.at[1], d_xsame)

    og_xp.start()
    og_core.start()
    pl.loop(MFIRST, NCH)(m_start)

    for cp in small:
        cp.wait()
    r = lax.broadcasted_iota(jnp.int32, (R1, R1), 0)
    c = lax.broadcasted_iota(jnp.int32, (R1, R1), 1)
    spread = jnp.where(2 * lax.rem(r, NCHIP) + r // NCHIP == c, jnp.broadcast_to(rin_ref[...].astype(F32), (R1, R1)), 0.0)
    rows_in = jnp.sum(spread, axis=1, keepdims=True).astype(jnp.int32)
    rows_out = as_column(rout_ref[...].astype(F32), R2).astype(jnp.int32)

    @pl.loop(0, NCH)
    def _(j):
        tile = quarter * NCH + j
        cols = lax.broadcasted_iota(jnp.int32, (R1, CH), 1) + tile * CH
        bit = jnp.bitwise_xor(parity(jnp.bitwise_and(rows_in, cols)), jnp.broadcast_to(sin_ref[tile], (R1, CH)))
        left_s[j] = (1 - 2 * bit).astype(F32).astype(BF16)

    for b in range(4):
        owner = col(2 * pair + b // 2, z, b % 2)
        cols = lax.broadcasted_iota(jnp.int32, (R2, C), 1) + owner * C
        bit = jnp.bitwise_xor(parity(jnp.bitwise_and(rows_out, cols)), jnp.broadcast_to(sout_ref[owner], (R2, C)))
        right_s[:, b * C:(b + 1) * C] = (1 - 2 * bit).astype(F32).astype(BF16)

    hacc[...] = jnp.zeros_like(hacc)
    sk[...] = jnp.zeros_like(sk)

    for t in range(FIRST[-1] + 6):
        def stage(step, body):
            for j in range(NCH):
                if FIRST[j] + step == t:
                    body(j)

        for s in (5, 4, 3, 2, 1):
            stage(s, a_step(s))
        stage(0, own_piece)
        stage(Y_OWN, y_own)
        for s in (5, 4, 3, 2, 1):
            stage(s - 1, b_step(s))
        stage(Y_OWN + 1, y_on)
        if t == OG_ON:
            og_forward()
        if t == OG_END:
            og_finish()
        stage(5, compute)

    for e in range(EX):
        h = hacc[e]
        hi = h.astype(BF16)
        rest = h - hi.astype(F32)
        mid = rest.astype(BF16)
        lo = (rest - mid.astype(F32)).astype(BF16)
        dims = (((1,), (1,)), ((), ()))
        part = lax.dot_general(lo, right_s[...], dims, preferred_element_type=F32)
        part = part + lax.dot_general(mid, right_s[...], dims, preferred_element_type=F32)
        part = part + lax.dot_general(hi, right_s[...], dims, preferred_element_type=F32)
        sk[:, e, :] = part

    to_core = remote(
        sk.at[pl.ds(pl.multiple_of((1 - core) * NCHIP, NCHIP), NCHIP)], sc, s_scs, s_sc, d_core
    )
    to_core.start()
    hops = sorted(((min(i, NX - i) + min(k, NZ - k), i, k) for i in range(NX) for k in range(NZ)), reverse=True)
    xt = [lax.rem(x + i, NX) * NZ for i in range(NX)]
    zt = [lax.rem(z + i, NZ) for i in range(NZ)]
    others = [xt[i] + zt[k] for _, i, k in hops if i or k]
    chip = me // 2
    to_core.wait()
    sc[...] += sk[pl.ds(pl.multiple_of(core * NCHIP, NCHIP), NCHIP)]
    for to in others:
        remote(sc.at[to], rs.at[chip], s_rss, s_rs, (y, to * 2 + core)).start()

    rs[chip] = sc[chip]
    some = rs.at[pl.ds(0, NCHIP - 1)]
    remote(some, some, s_rss, s_rs, d_core).wait_recv()
    rows_sum = jnp.sum(rs[...], axis=0)

    sq = as_row(jnp.sum(rows_sum * rows_sum, axis=1, keepdims=True), C)
    qs[...] = sq

    for to in others:
        for c_ in (1 - core, core):
            remote(qs, qr.at[me], s_qs, s_q, (y, to * 2 + c_)).start()
    remote(qs, qr.at[me], s_qs, s_q, d_core).start()

    qr[me] = sq
    someq = qr.at[pl.ds(0, NCOL - 1)]
    remote(someq, someq, s_qs, s_q, d_core).wait_recv()
    squares = as_column(jnp.sum(qr[...], axis=0), 8)
    unit = rows_sum * lax.rsqrt(squares / (R1 * R2) + 1e-06)

    tid = as_column(tid_ref[...].astype(F32), 8)
    wgt = as_column(w_ref[...].astype(F32), 8)

    def term(p):
        coef = jnp.where(tid == p.astype(F32), wgt, 0.0)
        return jnp.sum(coef * unit, axis=0, keepdims=True)

    def terms(g):
        return jnp.concatenate([term(PRO * g + i) for i in range(PRO)], axis=0)

    y_sends = []
    for k in range(1, NY):
        g = lax.rem(y + k, NY)
        ts[k - 1] = terms(g)
        cp = remote(ts.at[k - 1], yr.at[k - 1], s_tss.at[k - 1], s_t.at[k - 1], (g, me))
        cp.start()
        y_sends.append(cp)
    total = terms(y)
    for cp in y_sends:
        cp.wait()
    out_ref[...] = total + (yr[0] + yr[1] + yr[2])

    remote(some, some, s_rss, s_rs, d_core).wait_send()
    remote(someq, someq, s_qs, s_q, d_core).wait_send()
    og_core.wait_send()
    og_xp.wait_send()
    remote(ogb.at[2 * (1 - low) + core], ogb.at[2 * (1 - low) + core], s_ogs.at[2], s_og.at[2], d_core).wait_send()

    for j in range(NCH):
        for cp in x_sends(j):
            cp.wait_send()
        own_x(j, pair).wait_send()
        for n in range(6):
            b_x(j, n, pair, zcome(n // 2 + 1, n % 2)).wait_send()
        b_x(j, 6, pair, zcome(4, 0)).wait_send()
        for up in range(2):
            for s in range(1, 5):
                a_z(j, s, up, zback(s, up)).wait_send()
                b_z(j, s, up, zback(s, up)).wait_send()
        for a in range(2):
            m_core(j, a, blk).wait_send()
            for h in range(2):
                m_x(j, a, h).wait_send()
            for up in range(2):
                m_y(j, a, up, y, up).wait_send()
        m_y(j, 0, 2, ym, 0).wait_send()
        m_y(j, 1, 2, yp, 1).wait_send()


def body(
    inputs,
    out_grads,
    first_moment,
    second_moment,
    signs_in,
    signs_out,
    rows_in,
    rows_out,
    task_ids,
    weights,
):
    hbm = pl.BlockSpec(memory_space=pl.ANY)
    vmem = pl.BlockSpec(memory_space=pltpu.VMEM)
    dma = pltpu.SemaphoreType.DMA
    out = pl.pallas_call(
        kernel,
        out_shape=jax.ShapeDtypeStruct((PRO, C), F32),
        in_specs=[hbm] * 10,
        out_specs=vmem,
        scratch_shapes=[
            pltpu.VMEM((D // CH, 1, CH), jnp.int32),
            pltpu.VMEM((NCOL, 1, C), jnp.int32),
            pltpu.VMEM((1, R1), jnp.int32),
            pltpu.VMEM((1, R2), jnp.int32),
            pltpu.VMEM((1, EX), jnp.int32),
            pltpu.VMEM((1, EX), jnp.int32),
            dma((6,)),
            pltpu.VMEM((NCH, 4, EX, TK, CH), BF16),
            pltpu.VMEM((EX, 4 * TK, CH), F32),
            pltpu.VMEM((NCH, EX, 2, NZ, 4 * TK, CH), BF16),
            pltpu.VMEM((4, EX, 2, NZ, 2, 8, C), BF16),
            pltpu.VMEM((EX, 4 * C, 256), BF16),
            pltpu.VMEM((NCH, 4, CH, C), F32),
            pltpu.VMEM((NCH, 4, CH, C), F32),
            pltpu.VMEM((4 * C, CH), F32),
            pltpu.VMEM((4 * C, CH), F32),
            pltpu.VMEM((NCH, R1, CH), BF16),
            pltpu.VMEM((R2, 4 * C), BF16),
            pltpu.VMEM((EX, R1, 4 * C), F32),
            pltpu.VMEM((NCOL, 8, C), F32),
            pltpu.VMEM((NCHIP, 8, C), F32),
            pltpu.VMEM((NCHIP, 8, C), F32),
            pltpu.VMEM((1, C), F32),
            pltpu.VMEM((NCOL, 1, C), F32),
            pltpu.VMEM((NY - 1, PRO, C), F32),
            pltpu.VMEM((NY - 1, PRO, C), F32),
            dma((NCH, 4)), dma((NCH, 3)),
            dma((4,)), dma((3,)), dma((3,)),
            dma((NCH, 2)),
            dma((NCH, 2)), dma((NCH, 2)),
            dma((NCH, 2, 2)), dma((NCH, 2, 2)),
            dma((NCH, 2, 3)), dma((NCH, 2, 3)),
            dma((NCH,)), dma((NCH,)),
            dma((NCH, 2, 4)), dma((NCH, 2, 4)),
            dma((NCH, 2, 4)), dma((NCH, 2, 4)),
            dma((NCH, 7)), dma((NCH, 7)),
            dma, dma, dma, dma, dma, dma,
            dma((NY - 1,)), dma((NY - 1,)),
        ],
        compiler_params=pltpu.CompilerParams(
            collective_id=0, has_side_effects=True, vmem_limit_bytes=60 * 1024 * 1024
        ),
    )(
        inputs,
        out_grads.reshape(EX, 2, 2, NZ, 8, C),
        first_moment,
        second_moment,
        signs_in.reshape(D // CH, 1, CH),
        signs_out.reshape(NCOL, 1, C),
        rows_in.reshape(1, R1),
        rows_out.reshape(1, R2),
        task_ids.reshape(1, EX),
        weights.reshape(1, EX),
    )
    return out.reshape(PRO, 1, C)


def solution(mesh):
    placed = (
        P("grp", "col", None),
        P("grp", None, "col"),
        P(None, "col"),
        P(None, "col"),
        P(),
        P(),
        P(),
        P(),
        P("grp"),
        P("grp"),
    )
    return jax.shard_map(
        body, mesh=mesh, in_specs=placed, out_specs=P("grp", "col", None), check_vma=False
    )
```

```python
import functools
import math

import jax
import jax.numpy as jnp
from jax import lax
from jax.experimental import pallas as pl
from jax.experimental.pallas import tpu as pltpu
from jax.sharding import PartitionSpec as P

MESH = pl.DeviceIdType.MESH
F32 = jnp.float32
BF16 = jnp.bfloat16

NY = 4
NX = 4
NZ = 8
NCHIP = NX * NZ
NCOL = NCHIP * 2
EX = 6
TK = 4
D = 8192
QD = D // 4
CH = 256
NCH = QD // CH
MFIRST = 8
EA = (3, 2, 3, 2, 3, 2, 3, 2)
FIRST = (0, 0, 1, 1, 2, 2, 3, 3)
Y_OWN = 2
OG_ON = 4
OG_END = 5
SUB = CH // NY
C = 128
R1 = 64
R2 = 128
HALF = 128
PRO = 2

K_FM = 9.0 * math.sqrt(10.0)
K_G = math.sqrt(10.0)
K_SM = 999.0
K_EPS = 1e-8 * math.sqrt(1000.0)


def parity(both):
    for shift in (8, 4, 2, 1):
        both = jnp.bitwise_xor(both, jnp.right_shift(both, shift))
    return jnp.bitwise_and(both, 1)


def as_column(row, height):
    width = row.shape[1]
    r = lax.broadcasted_iota(jnp.int32, (height, width), 0)
    c = lax.broadcasted_iota(jnp.int32, (height, width), 1)
    return jnp.sum(jnp.where(r == c, jnp.broadcast_to(row, (height, width)), 0.0), axis=1, keepdims=True)


def as_row(column, width):
    height = column.shape[0]
    r = lax.broadcasted_iota(jnp.int32, (height, width), 0)
    c = lax.broadcasted_iota(jnp.int32, (height, width), 1)
    return jnp.sum(jnp.where(r == c, jnp.broadcast_to(column, (height, width)), 0.0), axis=0, keepdims=True)


def kernel(
    x_ref, og_ref, fm_ref, sm_ref, sin_hbm, sout_hbm, rin_hbm, rout_hbm, tid_hbm, w_hbm,
    out_ref,
    sin_ref, sout_ref, rin_ref, rout_ref, tid_ref, w_ref, s_small,
    rx, xs, xg, ogb, ogt, fmb, smb, ta, tb, left_s, right_s, hacc, sk, sc, rs, qs, qr, ts, yr,
    s_rx, s_rxs, s_ogl, s_og, s_ogs, s_ml, s_mc, s_mcs, s_mx, s_mxs, s_my, s_mys,
    s_ax, s_axs, s_az, s_azs, s_bz, s_bzs, s_bx, s_bxs,
    s_sc, s_scs, s_rs, s_rss, s_q, s_qs, s_t, s_tss,
):
    y = lax.axis_index("grp")
    me = lax.axis_index("col")
    core = lax.rem(me, 2)
    z = lax.rem(me // 2, NZ)
    x = me // (2 * NZ)
    pair = x // 2
    low = lax.rem(x, 2)
    cls = lax.rem(pair + low, 2)
    quarter = 2 * cls + core
    blk = 2 * low + core

    def col(x_, z_, c_):
        return (x_ * NZ + z_) * 2 + c_

    xpart = x + 1 - 2 * low
    cross = NX - 1 - x
    zp = lax.rem(z + 1, NZ)
    zm = lax.rem(z + NZ - 1, NZ)
    yp = lax.rem(y + 1, NY)
    ym = lax.rem(y + NY - 1, NY)
    d_core = (y, col(x, z, 1 - core))
    d_xp = tuple((y, col(xpart, z, c_)) for c_ in range(2))
    d_xsame = (y, col(xpart, z, core))
    d_cross = (y, col(cross, z, core))
    d_z = ((y, col(x, zp, core)), (y, col(x, zm, core)))
    d_y = ((yp, me), (ym, me))

    def remote(src, dst, ssem, rsem, dev):
        return pltpu.make_async_remote_copy(
            src_ref=src, dst_ref=dst, send_sem=ssem, recv_sem=rsem, device_id=dev, device_id_type=MESH
        )

    barrier = pltpu.get_barrier_semaphore()
    for dev in (d_core, *d_xp, d_cross, *d_z, *d_y):
        pl.semaphore_signal(barrier, inc=1, device_id=dev, device_id_type=MESH)

    og_local = []
    for p_ in range(2):
        for l_ in range(2):
            cp = pltpu.make_async_copy(og_ref.at[:, p_, l_], ogb.at[blk, :, p_, :, l_], s_ogl.at[2 * p_ + l_])
            cp.start()
            og_local.append(cp)
    def x_part(q, j):
        return x_ref.at[:, :, pl.ds(pl.multiple_of(q * QD + j * CH, CH), CH)]

    def x_local(j):
        return pltpu.make_async_copy(x_part(quarter, j), rx.at[j, blk], s_rx.at[j, blk])

    def x_sends(j):
        targets = ((d_xp[0], 2 * (1 - cls)), (d_xp[1], 2 * (1 - cls) + 1), (d_core, 2 * cls + 1 - core))
        return [remote(x_part(q, j), rx.at[j, blk], s_rxs.at[j, i], s_rx.at[j, blk], dev) for i, (dev, q) in enumerate(targets)]

    @pl.loop(0, NCH)
    def _(j):
        x_local(j).start()

    small = []
    for i, (src, dst) in enumerate(
        ((sin_hbm, sin_ref), (sout_hbm, sout_ref), (rin_hbm, rin_ref), (rout_hbm, rout_ref), (tid_hbm, tid_ref), (w_hbm, w_ref))
    ):
        cp = pltpu.make_async_copy(src, dst, s_small.at[i])
        cp.start()
        small.append(cp)
    pl.semaphore_wait(barrier, 8)

    @pl.loop(0, NCH)
    def _(j):
        for cp in x_sends(j):
            cp.start()

    def A(j):
        return slice(0, EA[j])

    def B(j):
        return slice(EA[j], EX)

    def zback(s, up):
        return lax.rem(z + NZ - (s - 1), NZ) if up == 0 else lax.rem(z + s - 1, NZ)

    def zcome(s, up):
        return lax.rem(z + NZ - s, NZ) if up == 0 else lax.rem(z + s, NZ)

    def own_x(j, where):
        v = xg.at[j, :, where, z]
        return remote(v, v, s_axs.at[j], s_ax.at[j], d_cross)

    def a_z(j, s, up, zz):
        v = xg.at[j, A(j), :, zz] if s < 4 else xg.at[j, A(j), :, zz, :, pl.ds(up * HALF, HALF)]
        return remote(v, v, s_azs.at[j, up, s - 1], s_az.at[j, up, s - 1], d_z[up])

    def b_z(j, s, up, zz):
        v = xg.at[j, B(j), pair, zz] if s < 4 else xg.at[j, B(j), pair, zz, :, pl.ds(up * HALF, HALF)]
        return remote(v, v, s_bzs.at[j, up, s - 1], s_bz.at[j, up, s - 1], d_z[up])

    def b_x(j, n, where, zz):
        v = xg.at[j, B(j), where, zz]
        return remote(v, v, s_bxs.at[j, n], s_bx.at[j, n], d_cross)

    moments = ((fm_ref, fmb), (sm_ref, smb))

    def rows(q, j, extra, n):
        return pl.ds(pl.multiple_of(q * QD + j * CH + extra, SUB), n)

    def m_local(j, a):
        return pltpu.make_async_copy(moments[a][0].at[rows(quarter, j, 0, CH)], moments[a][1].at[j, blk], s_ml.at[j, a])

    def m_core(j, a, b):
        q = 2 * cls + 1 - core
        return remote(moments[a][0].at[rows(q, j, 0, CH)], moments[a][1].at[j, b], s_mcs.at[j, a], s_mc.at[j, a], d_core)

    def m_x(j, a, h):
        q = 2 * (1 - cls) + h
        return remote(
            moments[a][0].at[rows(q, j, y * SUB, SUB)],
            moments[a][1].at[j, blk, pl.ds(pl.multiple_of(y * SUB, SUB), SUB)],
            s_mxs.at[j, a, h], s_mx.at[j, a, core], d_xp[h],
        )

    def m_x_come(j, a, h):
        v = moments[a][1].at[j, 2 * (1 - low) + h, pl.ds(pl.multiple_of(y * SUB, SUB), SUB)]
        return remote(v, v, s_mxs.at[j, a, h], s_mx.at[j, a, h], d_xp[h])

    def m_y(j, a, k, yy, up):
        v = moments[a][1].at[j, pl.ds(2 * (1 - low), 2), pl.ds(pl.multiple_of(yy * SUB, SUB), SUB)]
        return remote(v, v, s_mys.at[j, a, k], s_my.at[j, a, k], d_y[up])

    y2 = lax.rem(y + 2, NY)

    def m_start(j):
        for a in range(2):
            for h in range(2):
                m_x(j, a, h).start()
        for a in range(2):
            m_core(j, a, blk).start()
            m_local(j, a).start()

    def a_step(s):
        def go(j):
            if s == 1:
                own_x(j, 1 - pair).wait_recv()
            for up in range(2):
                if s > 1:
                    a_z(j, s - 1, up, zcome(s - 1, up)).wait_recv()
                if s < 5:
                    a_z(j, s, up, zback(s, up)).start()

        return go

    def b_step(s):
        def go(j):
            for up in range(2):
                if s > 1:
                    b_z(j, s - 1, up, zcome(s - 1, up)).wait_recv()
                if s < 5:
                    b_z(j, s, up, zback(s, up)).start()
                if 1 < s < 5:
                    b_x(j, 2 * (s - 2) + up, pair, zcome(s - 1, up)).start()
            if s == 5:
                b_x(j, 6, pair, zcome(4, 0)).start()

        return go

    def own_piece(j):
        for b in range(4):
            pltpu.make_async_copy(rx.at[j, b], rx.at[j, b], s_rx.at[j, b]).wait()
            xs[:, TK * b:TK * (b + 1), :] = rx[j, b].astype(F32)
        xg[j, :, pair, z] = xs[...].astype(BF16)
        own_x(j, pair).start()

    def y_own(j):
        for a in range(2):
            for h in range(2):
                m_x_come(j, a, h).wait_recv()
            for up in range(2):
                m_y(j, a, up, y, up).start()

    def y_on(j):
        m_y(j, 0, 0, ym, 0).wait_recv()
        m_y(j, 0, 2, ym, 0).start()
        m_y(j, 1, 1, yp, 1).wait_recv()
        m_y(j, 1, 2, yp, 1).start()

    def compute(j):
        for a in range(2):
            m_y(j, a, 1 - a, (yp, ym)[a], 1 - a).wait_recv()
            m_y(j, a, 2, y2, a).wait_recv()
            m_core(j, a, 2 * low + 1 - core).wait_recv()
            m_local(j, a).wait()
        for n in range(6):
            b_x(j, n, 1 - pair, zcome(n // 2 + 1, n % 2)).wait_recv()
        b_x(j, 6, 1 - pair, zcome(4, 0)).wait_recv()
        for b in range(4):
            ta[b * C:(b + 1) * C, :] = (fmb[j, b] * K_FM).T
            tb[b * C:(b + 1) * C, :] = (smb[j, b] * K_SM).T

        def one(e):
            acts = xg[j, e].reshape(2 * NZ * 4 * TK, CH)
            for h in range(2):
                sl = slice(h * 2 * C, (h + 1) * 2 * C)
                g = jnp.dot(ogt[e, sl, :], acts, preferred_element_type=F32)
                v = g * g + tb[sl, :]
                m = g * K_G + ta[sl, :]
                u = (m / (v * lax.rsqrt(v) + K_EPS)).astype(BF16)
                hacc[e, :, sl] += lax.dot_general(
                    left_s[j], u, (((1,), (1,)), ((), ())), preferred_element_type=F32
                )

        for e in range(EX):
            one(e)

    def og_forward():
        og_in = remote(ogb.at[2 * (1 - low) + core], ogb.at[2 * (1 - low) + core], s_ogs.at[1], s_og.at[1], d_xsame)
        og_in.wait_recv()
        remote(ogb.at[2 * (1 - low) + core], ogb.at[2 * (1 - low) + core], s_ogs.at[2], s_og.at[2], d_core).start()

    def og_finish():
        b1 = 2 * low + 1 - core
        b2 = 2 * (1 - low) + 1 - core
        remote(ogb.at[b1], ogb.at[b1], s_ogs.at[0], s_og.at[0], d_core).wait_recv()
        remote(ogb.at[b2], ogb.at[b2], s_ogs.at[2], s_og.at[2], d_core).wait_recv()

        @pl.loop(0, EX)
        def _(e):
            for b in range(4):
                v = ogb[b, e].astype(F32).reshape(4 * NZ * 8, C)
                ogt[e, b * C:(b + 1) * C, :] = v.T.astype(BF16)

    for t in range(FIRST[-1] + 6):
        def stage(step, body):
            for j in range(NCH):
                if FIRST[j] + step == t:
                    body(j)

        for s in (5, 4, 3, 2, 1):
            stage(s, a_step(s))
        stage(0, own_piece)
        stage(Y_OWN, y_own)
        for s in (5, 4, 3, 2, 1):
            stage(s - 1, b_step(s))
        stage(Y_OWN + 1, y_on)
        if t == 0:
            pl.loop(0, MFIRST)(m_start)
            for cp in og_local:
                cp.wait()
            og_core = remote(ogb.at[blk], ogb.at[blk], s_ogs.at[0], s_og.at[0], d_core)
            og_xp = remote(ogb.at[blk], ogb.at[blk], s_ogs.at[1], s_og.at[1], d_xsame)

            og_xp.start()
            og_core.start()
            pl.loop(MFIRST, NCH)(m_start)

        if t == 1:
            for cp in small:
                cp.wait()
            r = lax.broadcasted_iota(jnp.int32, (R1, R1), 0)
            c = lax.broadcasted_iota(jnp.int32, (R1, R1), 1)
            spread = jnp.where(2 * lax.rem(r, NCHIP) + r // NCHIP == c, jnp.broadcast_to(rin_ref[...].astype(F32), (R1, R1)), 0.0)
            rows_in = jnp.sum(spread, axis=1, keepdims=True).astype(jnp.int32)
            rows_out = as_column(rout_ref[...].astype(F32), R2).astype(jnp.int32)

            @pl.loop(0, NCH)
            def _(j):
                tile = quarter * NCH + j
                cols = lax.broadcasted_iota(jnp.int32, (R1, CH), 1) + tile * CH
                bit = jnp.bitwise_xor(parity(jnp.bitwise_and(rows_in, cols)), jnp.broadcast_to(sin_ref[tile], (R1, CH)))
                left_s[j] = (1 - 2 * bit).astype(F32).astype(BF16)

            for b in range(4):
                owner = col(2 * pair + b // 2, z, b % 2)
                cols = lax.broadcasted_iota(jnp.int32, (R2, C), 1) + owner * C
                bit = jnp.bitwise_xor(parity(jnp.bitwise_and(rows_out, cols)), jnp.broadcast_to(sout_ref[owner], (R2, C)))
                right_s[:, b * C:(b + 1) * C] = (1 - 2 * bit).astype(F32).astype(BF16)

            hacc[...] = jnp.zeros_like(hacc)
            sk[...] = jnp.zeros_like(sk)

        if t == OG_ON:
            og_forward()
        if t == OG_END:
            og_finish()
        stage(5, compute)

    for e in range(EX):
        h = hacc[e]
        hi = h.astype(BF16)
        rest = h - hi.astype(F32)
        mid = rest.astype(BF16)
        lo = (rest - mid.astype(F32)).astype(BF16)
        dims = (((1,), (1,)), ((), ()))
        part = lax.dot_general(lo, right_s[...], dims, preferred_element_type=F32)
        part = part + lax.dot_general(mid, right_s[...], dims, preferred_element_type=F32)
        part = part + lax.dot_general(hi, right_s[...], dims, preferred_element_type=F32)
        sk[:, e, :] = part

    to_core = remote(
        sk.at[pl.ds(pl.multiple_of((1 - core) * NCHIP, NCHIP), NCHIP)], sc, s_scs, s_sc, d_core
    )
    to_core.start()
    hops = sorted(((min(i, NX - i) + min(k, NZ - k), i, k) for i in range(NX) for k in range(NZ)), reverse=True)
    xt = [lax.rem(x + i, NX) * NZ for i in range(NX)]
    zt = [lax.rem(z + i, NZ) for i in range(NZ)]
    others = [xt[i] + zt[k] for _, i, k in hops if i or k]
    chip = me // 2
    to_core.wait()
    sc[...] += sk[pl.ds(pl.multiple_of(core * NCHIP, NCHIP), NCHIP)]
    for to in others:
        remote(sc.at[to], rs.at[chip], s_rss, s_rs, (y, to * 2 + core)).start()

    rs[chip] = sc[chip]
    tid = as_column(tid_ref[...].astype(F32), 8)
    wgt = as_column(w_ref[...].astype(F32), 8)

    og_core.wait_send()
    og_xp.wait_send()
    remote(ogb.at[2 * (1 - low) + core], ogb.at[2 * (1 - low) + core], s_ogs.at[2], s_og.at[2], d_core).wait_send()

    for j in range(NCH):
        for cp in x_sends(j):
            cp.wait_send()
        own_x(j, pair).wait_send()
        for n in range(6):
            b_x(j, n, pair, zcome(n // 2 + 1, n % 2)).wait_send()
        b_x(j, 6, pair, zcome(4, 0)).wait_send()
        for up in range(2):
            for s in range(1, 5):
                a_z(j, s, up, zback(s, up)).wait_send()
                b_z(j, s, up, zback(s, up)).wait_send()
        for a in range(2):
            m_core(j, a, blk).wait_send()
            for h in range(2):
                m_x(j, a, h).wait_send()
            for up in range(2):
                m_y(j, a, up, y, up).wait_send()
        m_y(j, 0, 2, ym, 0).wait_send()
        m_y(j, 1, 2, yp, 1).wait_send()

    some = rs.at[pl.ds(0, NCHIP - 1)]
    remote(some, some, s_rss, s_rs, d_core).wait_recv()
    rows_sum = jnp.sum(rs[...], axis=0)

    sq = as_row(jnp.sum(rows_sum * rows_sum, axis=1, keepdims=True), C)
    qs[...] = sq

    for to in others:
        for c_ in (1 - core, core):
            remote(qs, qr.at[me], s_qs, s_q, (y, to * 2 + c_)).start()
    remote(qs, qr.at[me], s_qs, s_q, d_core).start()

    qr[me] = sq
    someq = qr.at[pl.ds(0, NCOL - 1)]
    remote(someq, someq, s_qs, s_q, d_core).wait_recv()
    squares = as_column(jnp.sum(qr[...], axis=0), 8)
    unit = rows_sum * lax.rsqrt(squares / (R1 * R2) + 1e-06)


    def term(p):
        coef = jnp.where(tid == p.astype(F32), wgt, 0.0)
        return jnp.sum(coef * unit, axis=0, keepdims=True)

    def terms(g):
        return jnp.concatenate([term(PRO * g + i) for i in range(PRO)], axis=0)

    y_sends = []
    for k in range(1, NY):
        g = lax.rem(y + k, NY)
        ts[k - 1] = terms(g)
        cp = remote(ts.at[k - 1], yr.at[k - 1], s_tss.at[k - 1], s_t.at[k - 1], (g, me))
        cp.start()
        y_sends.append(cp)
    total = terms(y)
    for cp in y_sends:
        cp.wait()
    out_ref[...] = total + (yr[0] + yr[1] + yr[2])

    remote(some, some, s_rss, s_rs, d_core).wait_send()
    remote(someq, someq, s_qs, s_q, d_core).wait_send()


def body(
    inputs,
    out_grads,
    first_moment,
    second_moment,
    signs_in,
    signs_out,
    rows_in,
    rows_out,
    task_ids,
    weights,
):
    hbm = pl.BlockSpec(memory_space=pl.ANY)
    vmem = pl.BlockSpec(memory_space=pltpu.VMEM)
    dma = pltpu.SemaphoreType.DMA
    out = pl.pallas_call(
        kernel,
        out_shape=jax.ShapeDtypeStruct((PRO, C), F32),
        in_specs=[hbm] * 10,
        out_specs=vmem,
        scratch_shapes=[
            pltpu.VMEM((D // CH, 1, CH), jnp.int32),
            pltpu.VMEM((NCOL, 1, C), jnp.int32),
            pltpu.VMEM((1, R1), jnp.int32),
            pltpu.VMEM((1, R2), jnp.int32),
            pltpu.VMEM((1, EX), jnp.int32),
            pltpu.VMEM((1, EX), jnp.int32),
            dma((6,)),
            pltpu.VMEM((NCH, 4, EX, TK, CH), BF16),
            pltpu.VMEM((EX, 4 * TK, CH), F32),
            pltpu.VMEM((NCH, EX, 2, NZ, 4 * TK, CH), BF16),
            pltpu.VMEM((4, EX, 2, NZ, 2, 8, C), BF16),
            pltpu.VMEM((EX, 4 * C, 256), BF16),
            pltpu.VMEM((NCH, 4, CH, C), F32),
            pltpu.VMEM((NCH, 4, CH, C), F32),
            pltpu.VMEM((4 * C, CH), F32),
            pltpu.VMEM((4 * C, CH), F32),
            pltpu.VMEM((NCH, R1, CH), BF16),
            pltpu.VMEM((R2, 4 * C), BF16),
            pltpu.VMEM((EX, R1, 4 * C), F32),
            pltpu.VMEM((NCOL, 8, C), F32),
            pltpu.VMEM((NCHIP, 8, C), F32),
            pltpu.VMEM((NCHIP, 8, C), F32),
            pltpu.VMEM((1, C), F32),
            pltpu.VMEM((NCOL, 1, C), F32),
            pltpu.VMEM((NY - 1, PRO, C), F32),
            pltpu.VMEM((NY - 1, PRO, C), F32),
            dma((NCH, 4)), dma((NCH, 3)),
            dma((4,)), dma((3,)), dma((3,)),
            dma((NCH, 2)),
            dma((NCH, 2)), dma((NCH, 2)),
            dma((NCH, 2, 2)), dma((NCH, 2, 2)),
            dma((NCH, 2, 3)), dma((NCH, 2, 3)),
            dma((NCH,)), dma((NCH,)),
            dma((NCH, 2, 4)), dma((NCH, 2, 4)),
            dma((NCH, 2, 4)), dma((NCH, 2, 4)),
            dma((NCH, 7)), dma((NCH, 7)),
            dma, dma, dma, dma, dma, dma,
            dma((NY - 1,)), dma((NY - 1,)),
        ],
        compiler_params=pltpu.CompilerParams(
            collective_id=0, has_side_effects=True, vmem_limit_bytes=60 * 1024 * 1024
        ),
    )(
        inputs,
        out_grads.reshape(EX, 2, 2, NZ, 8, C),
        first_moment,
        second_moment,
        signs_in.reshape(D // CH, 1, CH),
        signs_out.reshape(NCOL, 1, C),
        rows_in.reshape(1, R1),
        rows_out.reshape(1, R2),
        task_ids.reshape(1, EX),
        weights.reshape(1, EX),
    )
    return out.reshape(PRO, 1, C)


def solution(mesh):
    placed = (
        P("grp", "col", None),
        P("grp", None, "col"),
        P(None, "col"),
        P(None, "col"),
        P(),
        P(),
        P(),
        P(),
        P("grp"),
        P("grp"),
    )
    return jax.shard_map(
        body, mesh=mesh, in_specs=placed, out_specs=P("grp", "col", None), check_vma=False
    )
```

```python
import functools
import math

import jax
import jax.numpy as jnp
from jax import lax
from jax.experimental import pallas as pl
from jax.experimental.pallas import tpu as pltpu
from jax.sharding import PartitionSpec as P

MESH = pl.DeviceIdType.MESH
F32 = jnp.float32
BF16 = jnp.bfloat16

NY = 4
NX = 4
NZ = 8
NCHIP = NX * NZ
NCOL = NCHIP * 2
EX = 6
TK = 4
D = 8192
QD = D // 4
CH = 256
NCH = QD // CH
MFIRST = 8
EA = (3, 2, 3, 2, 3, 2, 3, 2)
FIRST = (0, 0, 1, 1, 2, 2, 3, 3)
Y_OWN = 2
OG_ON = 4
OG_END = 5
SUB = CH // NY
C = 128
R1 = 64
R2 = 128
HALF = 128
PRO = 2

K_FM = 9.0 * math.sqrt(10.0)
K_G = math.sqrt(10.0)
K_SM = 999.0
K_EPS = 1e-8 * math.sqrt(1000.0)


def parity(both):
    for shift in (8, 4, 2, 1):
        both = jnp.bitwise_xor(both, jnp.right_shift(both, shift))
    return jnp.bitwise_and(both, 1)


def as_column(row, height):
    width = row.shape[1]
    r = lax.broadcasted_iota(jnp.int32, (height, width), 0)
    c = lax.broadcasted_iota(jnp.int32, (height, width), 1)
    return jnp.sum(jnp.where(r == c, jnp.broadcast_to(row, (height, width)), 0.0), axis=1, keepdims=True)


def as_row(column, width):
    height = column.shape[0]
    r = lax.broadcasted_iota(jnp.int32, (height, width), 0)
    c = lax.broadcasted_iota(jnp.int32, (height, width), 1)
    return jnp.sum(jnp.where(r == c, jnp.broadcast_to(column, (height, width)), 0.0), axis=0, keepdims=True)


def kernel(
    x_ref, og_ref, fm_ref, sm_ref, sin_hbm, sout_hbm, rin_hbm, rout_hbm, tid_hbm, w_hbm,
    out_ref,
    sin_ref, sout_ref, rin_ref, rout_ref, tid_ref, w_ref, s_small,
    rx, xs, xg, ogb, ogt, fmb, smb, ta, tb, left_s, right_s, hacc, sk, sc, rs, qs, qr, ts, yr,
    s_rx, s_rxs, s_ogl, s_og, s_ogs, s_ml, s_mc, s_mcs, s_mx, s_mxs, s_my, s_mys,
    s_ax, s_axs, s_az, s_azs, s_bz, s_bzs, s_bx, s_bxs,
    s_sc, s_scs, s_rs, s_rss, s_q, s_qs, s_t, s_tss,
):
    y = lax.axis_index("grp")
    me = lax.axis_index("col")
    core = lax.rem(me, 2)
    z = lax.rem(me // 2, NZ)
    x = me // (2 * NZ)
    pair = x // 2
    low = lax.rem(x, 2)
    cls = lax.rem(pair + low, 2)
    quarter = 2 * cls + core
    blk = 2 * low + core

    def col(x_, z_, c_):
        return (x_ * NZ + z_) * 2 + c_

    xpart = x + 1 - 2 * low
    cross = NX - 1 - x
    zp = lax.rem(z + 1, NZ)
    zm = lax.rem(z + NZ - 1, NZ)
    yp = lax.rem(y + 1, NY)
    ym = lax.rem(y + NY - 1, NY)
    d_core = (y, col(x, z, 1 - core))
    d_xp = tuple((y, col(xpart, z, c_)) for c_ in range(2))
    d_xsame = (y, col(xpart, z, core))
    d_cross = (y, col(cross, z, core))
    d_z = ((y, col(x, zp, core)), (y, col(x, zm, core)))
    d_y = ((yp, me), (ym, me))

    def remote(src, dst, ssem, rsem, dev):
        return pltpu.make_async_remote_copy(
            src_ref=src, dst_ref=dst, send_sem=ssem, recv_sem=rsem, device_id=dev, device_id_type=MESH
        )

    barrier = pltpu.get_barrier_semaphore()
    for dev in (d_core, *d_xp, d_cross, *d_z, *d_y):
        pl.semaphore_signal(barrier, inc=1, device_id=dev, device_id_type=MESH)

    og_local = []
    for p_ in range(2):
        for l_ in range(2):
            cp = pltpu.make_async_copy(og_ref.at[:, p_, l_], ogb.at[blk, :, p_, :, l_], s_ogl.at[2 * p_ + l_])
            cp.start()
            og_local.append(cp)
    def x_part(q, j):
        return x_ref.at[:, :, pl.ds(pl.multiple_of(q * QD + j * CH, CH), CH)]

    def x_local(j):
        return pltpu.make_async_copy(x_part(quarter, j), rx.at[j, blk], s_rx.at[j, blk])

    def x_sends(j):
        targets = ((d_xp[0], 2 * (1 - cls)), (d_xp[1], 2 * (1 - cls) + 1), (d_core, 2 * cls + 1 - core))
        return [remote(x_part(q, j), rx.at[j, blk], s_rxs.at[j, i], s_rx.at[j, blk], dev) for i, (dev, q) in enumerate(targets)]

    @pl.loop(0, NCH)
    def _(j):
        x_local(j).start()

    small = []
    for i, (src, dst) in enumerate(
        ((sin_hbm, sin_ref), (sout_hbm, sout_ref), (rin_hbm, rin_ref), (rout_hbm, rout_ref), (tid_hbm, tid_ref), (w_hbm, w_ref))
    ):
        cp = pltpu.make_async_copy(src, dst, s_small.at[i])
        cp.start()
        small.append(cp)
    pl.semaphore_wait(barrier, 8)

    @pl.loop(0, NCH)
    def _(j):
        for cp in x_sends(j):
            cp.start()

    def A(j):
        return slice(0, EA[j])

    def B(j):
        return slice(EA[j], EX)

    def zback(s, up):
        return lax.rem(z + NZ - (s - 1), NZ) if up == 0 else lax.rem(z + s - 1, NZ)

    def zcome(s, up):
        return lax.rem(z + NZ - s, NZ) if up == 0 else lax.rem(z + s, NZ)

    def own_x(j, where):
        v = xg.at[j, :, where, z]
        return remote(v, v, s_axs.at[j], s_ax.at[j], d_cross)

    def a_z(j, s, up, zz):
        v = xg.at[j, A(j), :, zz] if s < 4 else xg.at[j, A(j), :, zz, :, pl.ds(up * HALF, HALF)]
        return remote(v, v, s_azs.at[j, up, s - 1], s_az.at[j, up, s - 1], d_z[up])

    def b_z(j, s, up, zz):
        v = xg.at[j, B(j), pair, zz] if s < 4 else xg.at[j, B(j), pair, zz, :, pl.ds(up * HALF, HALF)]
        return remote(v, v, s_bzs.at[j, up, s - 1], s_bz.at[j, up, s - 1], d_z[up])

    def b_x(j, n, where, zz):
        v = xg.at[j, B(j), where, zz]
        return remote(v, v, s_bxs.at[j, n], s_bx.at[j, n], d_cross)

    moments = ((fm_ref, fmb), (sm_ref, smb))

    def rows(q, j, extra, n):
        return pl.ds(pl.multiple_of(q * QD + j * CH + extra, SUB), n)

    def m_local(j, a):
        return pltpu.make_async_copy(moments[a][0].at[rows(quarter, j, 0, CH)], moments[a][1].at[j, blk], s_ml.at[j, a])

    def m_core(j, a, b):
        q = 2 * cls + 1 - core
        return remote(moments[a][0].at[rows(q, j, 0, CH)], moments[a][1].at[j, b], s_mcs.at[j, a], s_mc.at[j, a], d_core)

    def m_x(j, a, h):
        q = 2 * (1 - cls) + h
        return remote(
            moments[a][0].at[rows(q, j, y * SUB, SUB)],
            moments[a][1].at[j, blk, pl.ds(pl.multiple_of(y * SUB, SUB), SUB)],
            s_mxs.at[j, a, h], s_mx.at[j, a, core], d_xp[h],
        )

    def m_x_come(j, a, h):
        v = moments[a][1].at[j, 2 * (1 - low) + h, pl.ds(pl.multiple_of(y * SUB, SUB), SUB)]
        return remote(v, v, s_mxs.at[j, a, h], s_mx.at[j, a, h], d_xp[h])

    def m_y(j, a, k, yy, up):
        v = moments[a][1].at[j, pl.ds(2 * (1 - low), 2), pl.ds(pl.multiple_of(yy * SUB, SUB), SUB)]
        return remote(v, v, s_mys.at[j, a, k], s_my.at[j, a, k], d_y[up])

    y2 = lax.rem(y + 2, NY)

    def m_start(j):
        for a in range(2):
            for h in range(2):
                m_x(j, a, h).start()
        for a in range(2):
            m_core(j, a, blk).start()
            m_local(j, a).start()

    def a_step(s):
        def go(j):
            if s == 1:
                own_x(j, 1 - pair).wait_recv()
            for up in range(2):
                if s > 1:
                    a_z(j, s - 1, up, zcome(s - 1, up)).wait_recv()
                if s < 5:
                    a_z(j, s, up, zback(s, up)).start()

        return go

    def b_step(s):
        def go(j):
            for up in range(2):
                if s > 1:
                    b_z(j, s - 1, up, zcome(s - 1, up)).wait_recv()
                if s < 5:
                    b_z(j, s, up, zback(s, up)).start()
                if 1 < s < 5:
                    b_x(j, 2 * (s - 2) + up, pair, zcome(s - 1, up)).start()
            if s == 5:
                b_x(j, 6, pair, zcome(4, 0)).start()

        return go

    def own_piece(j):
        for b in range(4):
            pltpu.make_async_copy(rx.at[j, b], rx.at[j, b], s_rx.at[j, b]).wait()
            xs[:, TK * b:TK * (b + 1), :] = rx[j, b].astype(F32)
        xg[j, :, pair, z] = xs[...].astype(BF16)
        own_x(j, pair).start()

    def y_own(j):
        for a in range(2):
            for h in range(2):
                m_x_come(j, a, h).wait_recv()
            for up in range(2):
                m_y(j, a, up, y, up).start()

    def y_on(j):
        m_y(j, 0, 0, ym, 0).wait_recv()
        m_y(j, 0, 2, ym, 0).start()
        m_y(j, 1, 1, yp, 1).wait_recv()
        m_y(j, 1, 2, yp, 1).start()

    def compute(j):
        for a in range(2):
            m_y(j, a, 1 - a, (yp, ym)[a], 1 - a).wait_recv()
            m_y(j, a, 2, y2, a).wait_recv()
            m_core(j, a, 2 * low + 1 - core).wait_recv()
            m_local(j, a).wait()
        for n in range(6):
            b_x(j, n, 1 - pair, zcome(n // 2 + 1, n % 2)).wait_recv()
        b_x(j, 6, 1 - pair, zcome(4, 0)).wait_recv()
        for b in range(4):
            ta[b * C:(b + 1) * C, :] = (fmb[j, b] * K_FM).T
            tb[b * C:(b + 1) * C, :] = (smb[j, b] * K_SM).T

        def one(e):
            acts = xg[j, e].reshape(2 * NZ * 4 * TK, CH)
            for h in range(2):
                sl = slice(h * 2 * C, (h + 1) * 2 * C)
                g = jnp.dot(ogt[e, sl, :], acts, preferred_element_type=F32)
                v = g * g + tb[sl, :]
                m = g * K_G + ta[sl, :]
                u = (m / (v * lax.rsqrt(v) + K_EPS)).astype(BF16)
                hacc[e, :, sl] += lax.dot_general(
                    left_s[j], u, (((1,), (1,)), ((), ())), preferred_element_type=F32
                )

        for e in range(EX):
            one(e)

    def og_forward():
        og_in = remote(ogb.at[2 * (1 - low) + core], ogb.at[2 * (1 - low) + core], s_ogs.at[1], s_og.at[1], d_xsame)
        og_in.wait_recv()
        remote(ogb.at[2 * (1 - low) + core], ogb.at[2 * (1 - low) + core], s_ogs.at[2], s_og.at[2], d_core).start()

    def og_finish():
        b1 = 2 * low + 1 - core
        b2 = 2 * (1 - low) + 1 - core
        remote(ogb.at[b1], ogb.at[b1], s_ogs.at[0], s_og.at[0], d_core).wait_recv()
        remote(ogb.at[b2], ogb.at[b2], s_ogs.at[2], s_og.at[2], d_core).wait_recv()

        @pl.loop(0, EX)
        def _(e):
            for b in range(4):
                v = ogb[b, e].astype(F32).reshape(4 * NZ * 8, C)
                ogt[e, b * C:(b + 1) * C, :] = v.T.astype(BF16)

    for t in range(FIRST[-1] + 6):
        def stage(step, body):
            for j in range(NCH):
                if FIRST[j] + step == t:
                    body(j)

        for s in (5, 4, 3, 2, 1):
            stage(s, a_step(s))
        stage(0, own_piece)
        for s in (5, 4, 3, 2, 1):
            stage(s - 1, b_step(s))
        stage(Y_OWN + 1, y_on)
        stage(Y_OWN, y_own)
        if t == 0:
            pl.loop(0, MFIRST)(m_start)
            for cp in og_local:
                cp.wait()
            og_core = remote(ogb.at[blk], ogb.at[blk], s_ogs.at[0], s_og.at[0], d_core)
            og_xp = remote(ogb.at[blk], ogb.at[blk], s_ogs.at[1], s_og.at[1], d_xsame)

            og_xp.start()
            og_core.start()
            pl.loop(MFIRST, NCH)(m_start)

        if t == 1:
            for cp in small:
                cp.wait()
            r = lax.broadcasted_iota(jnp.int32, (R1, R1), 0)
            c = lax.broadcasted_iota(jnp.int32, (R1, R1), 1)
            spread = jnp.where(2 * lax.rem(r, NCHIP) + r // NCHIP == c, jnp.broadcast_to(rin_ref[...].astype(F32), (R1, R1)), 0.0)
            rows_in = jnp.sum(spread, axis=1, keepdims=True).astype(jnp.int32)
            rows_out = as_column(rout_ref[...].astype(F32), R2).astype(jnp.int32)

            @pl.loop(0, NCH)
            def _(j):
                tile = quarter * NCH + j
                cols = lax.broadcasted_iota(jnp.int32, (R1, CH), 1) + tile * CH
                bit = jnp.bitwise_xor(parity(jnp.bitwise_and(rows_in, cols)), jnp.broadcast_to(sin_ref[tile], (R1, CH)))
                left_s[j] = (1 - 2 * bit).astype(F32).astype(BF16)

            for b in range(4):
                owner = col(2 * pair + b // 2, z, b % 2)
                cols = lax.broadcasted_iota(jnp.int32, (R2, C), 1) + owner * C
                bit = jnp.bitwise_xor(parity(jnp.bitwise_and(rows_out, cols)), jnp.broadcast_to(sout_ref[owner], (R2, C)))
                right_s[:, b * C:(b + 1) * C] = (1 - 2 * bit).astype(F32).astype(BF16)

            hacc[...] = jnp.zeros_like(hacc)
            sk[...] = jnp.zeros_like(sk)

        if t == OG_ON:
            og_forward()
        if t == OG_END:
            og_finish()
        stage(5, compute)

    for e in range(EX):
        h = hacc[e]
        hi = h.astype(BF16)
        rest = h - hi.astype(F32)
        mid = rest.astype(BF16)
        lo = (rest - mid.astype(F32)).astype(BF16)
        dims = (((1,), (1,)), ((), ()))
        part = lax.dot_general(lo, right_s[...], dims, preferred_element_type=F32)
        part = part + lax.dot_general(mid, right_s[...], dims, preferred_element_type=F32)
        part = part + lax.dot_general(hi, right_s[...], dims, preferred_element_type=F32)
        sk[:, e, :] = part

    to_core = remote(
        sk.at[pl.ds(pl.multiple_of((1 - core) * NCHIP, NCHIP), NCHIP)], sc, s_scs, s_sc, d_core
    )
    to_core.start()
    hops = sorted(((min(i, NX - i) + min(k, NZ - k), i, k) for i in range(NX) for k in range(NZ)), reverse=True)
    xt = [lax.rem(x + i, NX) * NZ for i in range(NX)]
    zt = [lax.rem(z + i, NZ) for i in range(NZ)]
    others = [xt[i] + zt[k] for _, i, k in hops if i or k]
    chip = me // 2
    to_core.wait()
    sc[...] += sk[pl.ds(pl.multiple_of(core * NCHIP, NCHIP), NCHIP)]
    for to in others:
        remote(sc.at[to], rs.at[chip], s_rss, s_rs, (y, to * 2 + core)).start()

    rs[chip] = sc[chip]
    tid = as_column(tid_ref[...].astype(F32), 8)
    wgt = as_column(w_ref[...].astype(F32), 8)

    og_core.wait_send()
    og_xp.wait_send()
    remote(ogb.at[2 * (1 - low) + core], ogb.at[2 * (1 - low) + core], s_ogs.at[2], s_og.at[2], d_core).wait_send()

    for j in range(NCH):
        for cp in x_sends(j):
            cp.wait_send()
        own_x(j, pair).wait_send()
        for n in range(6):
            b_x(j, n, pair, zcome(n // 2 + 1, n % 2)).wait_send()
        b_x(j, 6, pair, zcome(4, 0)).wait_send()
        for up in range(2):
            for s in range(1, 5):
                a_z(j, s, up, zback(s, up)).wait_send()
                b_z(j, s, up, zback(s, up)).wait_send()
        for a in range(2):
            m_core(j, a, blk).wait_send()
            for h in range(2):
                m_x(j, a, h).wait_send()
            for up in range(2):
                m_y(j, a, up, y, up).wait_send()
        m_y(j, 0, 2, ym, 0).wait_send()
        m_y(j, 1, 2, yp, 1).wait_send()

    some = rs.at[pl.ds(0, NCHIP - 1)]
    remote(some, some, s_rss, s_rs, d_core).wait_recv()
    rows_sum = jnp.sum(rs[...], axis=0)

    sq = as_row(jnp.sum(rows_sum * rows_sum, axis=1, keepdims=True), C)
    qs[...] = sq

    for to in others:
        for c_ in (1 - core, core):
            remote(qs, qr.at[me], s_qs, s_q, (y, to * 2 + c_)).start()
    remote(qs, qr.at[me], s_qs, s_q, d_core).start()

    qr[me] = sq
    someq = qr.at[pl.ds(0, NCOL - 1)]
    remote(someq, someq, s_qs, s_q, d_core).wait_recv()
    squares = as_column(jnp.sum(qr[...], axis=0), 8)
    unit = rows_sum * lax.rsqrt(squares / (R1 * R2) + 1e-06)


    def term(p):
        coef = jnp.where(tid == p.astype(F32), wgt, 0.0)
        return jnp.sum(coef * unit, axis=0, keepdims=True)

    def terms(g):
        return jnp.concatenate([term(PRO * g + i) for i in range(PRO)], axis=0)

    y_sends = []
    for k in range(1, NY):
        g = lax.rem(y + k, NY)
        ts[k - 1] = terms(g)
        cp = remote(ts.at[k - 1], yr.at[k - 1], s_tss.at[k - 1], s_t.at[k - 1], (g, me))
        cp.start()
        y_sends.append(cp)
    total = terms(y)
    for cp in y_sends:
        cp.wait()
    out_ref[...] = total + (yr[0] + yr[1] + yr[2])

    remote(some, some, s_rss, s_rs, d_core).wait_send()
    remote(someq, someq, s_qs, s_q, d_core).wait_send()


def body(
    inputs,
    out_grads,
    first_moment,
    second_moment,
    signs_in,
    signs_out,
    rows_in,
    rows_out,
    task_ids,
    weights,
):
    hbm = pl.BlockSpec(memory_space=pl.ANY)
    vmem = pl.BlockSpec(memory_space=pltpu.VMEM)
    dma = pltpu.SemaphoreType.DMA
    out = pl.pallas_call(
        kernel,
        out_shape=jax.ShapeDtypeStruct((PRO, C), F32),
        in_specs=[hbm] * 10,
        out_specs=vmem,
        scratch_shapes=[
            pltpu.VMEM((D // CH, 1, CH), jnp.int32),
            pltpu.VMEM((NCOL, 1, C), jnp.int32),
            pltpu.VMEM((1, R1), jnp.int32),
            pltpu.VMEM((1, R2), jnp.int32),
            pltpu.VMEM((1, EX), jnp.int32),
            pltpu.VMEM((1, EX), jnp.int32),
            dma((6,)),
            pltpu.VMEM((NCH, 4, EX, TK, CH), BF16),
            pltpu.VMEM((EX, 4 * TK, CH), F32),
            pltpu.VMEM((NCH, EX, 2, NZ, 4 * TK, CH), BF16),
            pltpu.VMEM((4, EX, 2, NZ, 2, 8, C), BF16),
            pltpu.VMEM((EX, 4 * C, 256), BF16),
            pltpu.VMEM((NCH, 4, CH, C), F32),
            pltpu.VMEM((NCH, 4, CH, C), F32),
            pltpu.VMEM((4 * C, CH), F32),
            pltpu.VMEM((4 * C, CH), F32),
            pltpu.VMEM((NCH, R1, CH), BF16),
            pltpu.VMEM((R2, 4 * C), BF16),
            pltpu.VMEM((EX, R1, 4 * C), F32),
            pltpu.VMEM((NCOL, 8, C), F32),
            pltpu.VMEM((NCHIP, 8, C), F32),
            pltpu.VMEM((NCHIP, 8, C), F32),
            pltpu.VMEM((1, C), F32),
            pltpu.VMEM((NCOL, 1, C), F32),
            pltpu.VMEM((NY - 1, PRO, C), F32),
            pltpu.VMEM((NY - 1, PRO, C), F32),
            dma((NCH, 4)), dma((NCH, 3)),
            dma((4,)), dma((3,)), dma((3,)),
            dma((NCH, 2)),
            dma((NCH, 2)), dma((NCH, 2)),
            dma((NCH, 2, 2)), dma((NCH, 2, 2)),
            dma((NCH, 2, 3)), dma((NCH, 2, 3)),
            dma((NCH,)), dma((NCH,)),
            dma((NCH, 2, 4)), dma((NCH, 2, 4)),
            dma((NCH, 2, 4)), dma((NCH, 2, 4)),
            dma((NCH, 7)), dma((NCH, 7)),
            dma, dma, dma, dma, dma, dma,
            dma((NY - 1,)), dma((NY - 1,)),
        ],
        compiler_params=pltpu.CompilerParams(
            collective_id=0, has_side_effects=True, vmem_limit_bytes=60 * 1024 * 1024
        ),
    )(
        inputs,
        out_grads.reshape(EX, 2, 2, NZ, 8, C),
        first_moment,
        second_moment,
        signs_in.reshape(D // CH, 1, CH),
        signs_out.reshape(NCOL, 1, C),
        rows_in.reshape(1, R1),
        rows_out.reshape(1, R2),
        task_ids.reshape(1, EX),
        weights.reshape(1, EX),
    )
    return out.reshape(PRO, 1, C)


def solution(mesh):
    placed = (
        P("grp", "col", None),
        P("grp", None, "col"),
        P(None, "col"),
        P(None, "col"),
        P(),
        P(),
        P(),
        P(),
        P("grp"),
        P("grp"),
    )
    return jax.shard_map(
        body, mesh=mesh, in_specs=placed, out_specs=P("grp", "col", None), check_vma=False
    )
```
